32 devices in a mesh: depth: 4 (over z), row: 4 (over x, core), col: 2 (over y).
Axes of the slice: x: 2, y: 2, z: 4, core: 2. Of those that a mesh axis runs over, the one named last changes fastest.
Arguments:
- acts: bfloat16 [2048, 4096], P(('depth', 'col'), 'row'), may hold values from -0.3125 to 0.3125
- grad_out: bfloat16 [2048, 14336], P(('depth', 'row'), 'col'), may hold values from -6 to 6
- weight: bfloat16 [4096, 14336], P('row', 'col'), may hold values from -0.046875 to 0.046875
Outputs:
- grad_acts: bfloat16 [2048, 4096], P(('depth', 'col'), 'row')
- grad_weight: bfloat16 [4096, 14336], P('row', 'col')
The draws below stay inside these ranges and needn't reach their ends.
All inputs are finite; a program needn't handle non-finite values.
Results may differ from the reference program's by a relative error of at most 0.013.
Values may be sent and summed in bfloat16 or wider, within the bound.
A program may use at most 128 MiB of HBM per device.

```python
import jax
import jax.numpy as jnp

D = 4096
F = 14336
TOKENS = 2048
N_DEPTH = 4
N_COL = 2


def level_of(own_key, dims, cuts, low, high):
    loudness, own = 1.0, jax.random.fold_in(own_key, 6)
    for axis_at, shards_of in cuts:
        heights = jnp.exp(jax.random.uniform(jax.random.fold_in(own, axis_at), (shards_of,), jnp.float32, low / len(cuts), high / len(cuts)))
        loudness = loudness * jnp.repeat(heights, dims[axis_at] // shards_of).reshape([-1 if axis == axis_at else 1 for axis in range(len(dims))])
    return loudness


def gaussian(stream_key, dims, width, most, pieces=(), held_as=jnp.bfloat16):
    gain = level_of(stream_key, dims, pieces, -0.22, 0.18) if pieces else 1.0
    array = jax.random.normal(stream_key, dims, jnp.float32) * width * gain
    return jnp.minimum(jnp.maximum(array, -most), most).astype(held_as)


def setup_inputs(seed: int = 0) -> dict:
    splits = jax.random.split(jax.random.key(seed), 4)
    return {
        "acts": gaussian(splits[0], (TOKENS, D), (TOKENS ** -0.5), 0.3125, ((0, 8), (1, 4))),
        "grad_out": gaussian(splits[1], (TOKENS, F), 1.0, 6.0, ((0, 16), (1, 2))),
        "weight": gaussian(splits[2], (D, F), F ** -0.5, 0.046875, ((0, 4), (1, 2))),
    }


def reference(acts, grad_out, weight):
    block = F // N_COL
    grad_acts = jnp.zeros((TOKENS, D), jnp.float32)
    for index in range(N_COL):
        piece = grad_out[:, index * block:(index + 1) * block]
        wpart = weight[:, index * block:(index + 1) * block]
        term = jnp.dot(piece, wpart.T, preferred_element_type=jnp.float32).astype(jnp.bfloat16)
        grad_acts = grad_acts + term.astype(jnp.float32)
    layer = TOKENS // N_DEPTH
    grad_weight = jnp.zeros((D, F), jnp.float32)
    for index in range(N_DEPTH):
        rows_a = acts[index * layer:(index + 1) * layer]
        rows_g = grad_out[index * layer:(index + 1) * layer]
        term = jnp.dot(rows_a.T, rows_g, preferred_element_type=jnp.float32).astype(jnp.bfloat16)
        grad_weight = grad_weight + term.astype(jnp.float32)
    return grad_acts.astype(jnp.bfloat16), grad_weight.astype(jnp.bfloat16)
```

```python
import functools

import jax
import jax.numpy as jnp
from jax import lax
from jax.experimental import pallas as pl
from jax.experimental.pallas import tpu as pltpu
from jax.sharding import PartitionSpec as P

MESH = pl.DeviceIdType.MESH
CORES = 2


def lag(nd, nch, sub):
    per = nch + sub
    need = [per * (d - 1) + sub + 1 + nch - 1 - (nch * d + nch - 1) for d in range(1, nd)]
    need += [per * (nd - 2) + sub + 1 - (nch * (nd - 1) + 2)]
    return max(0, *need)


def kernel(nd, nr, nc, nch, cols, sub, a_ref, g_ref, w_ref, ga_ref, gw_ref,
           grads, acts, own_a, total, term, parts, wbuf,
           recv_g, recv_a, recv_t, send_g, send_a, send_t, load_sem, w_sem):
    nx = nr // CORES
    l, r, c = lax.axis_index("depth"), lax.axis_index("row"), lax.axis_index("col")
    core = lax.rem(r, CORES)
    xi = lax.div(r, CORES)
    partner = xi * CORES + (1 - core)
    xpeers = [lax.rem(xi + o, nx) * CORES + core for o in range(1, nx)]
    cpeers = [lax.rem(c + o, nc) for o in range(1, nc)]
    rows = g_ref.shape[0]
    width, feats = a_ref.shape
    layer = nr * rows
    block = layer // nc
    fsub = feats // sub
    per = nch + sub
    late = lag(nd, nch, sub)
    pairs = jnp.minimum(l, nd - 1 - l)
    far_up = l < nd // 2
    last = jnp.where(far_up, nd - 1, 0)
    first = jnp.where(far_up, 0, layer)
    UP, DOWN, CORE, X = 0, 1, 2, 3

    def piece(p, j):
        return grads.at[j, pl.ds(pl.multiple_of(p * rows, rows), rows), :]

    def whole(p):
        return grads.at[:, pl.ds(pl.multiple_of(p * rows, rows), rows), :]

    def apiece(q, i):
        return acts.at[pl.ds(pl.multiple_of(i * fsub, fsub), fsub), pl.ds(pl.multiple_of(q * width, width), width)]

    def awhole(q):
        return acts.at[:, pl.ds(pl.multiple_of(q * width, width), width)]

    def g_copy(p, j, way, dev):
        return pltpu.make_async_remote_copy(
            src_ref=piece(p, j), dst_ref=piece(p, j), send_sem=send_g.at[way, p],
            recv_sem=recv_g.at[p, j], device_id=dev, device_id_type=MESH)

    def a_copy(q, i, way, dev):
        return pltpu.make_async_remote_copy(
            src_ref=apiece(q, i), dst_ref=apiece(q, i), send_sem=send_a.at[way, q],
            recv_sem=recv_a.at[q, i], device_id=dev, device_id_type=MESH)

    def g_wait(p, j):
        pltpu.make_async_copy(piece(p, j), piece(p, j), recv_g.at[p, j]).wait()

    def a_wait(q, i):
        pltpu.make_async_copy(apiece(q, i), apiece(q, i), recv_a.at[q, i]).wait()

    def to_x(p, j):
        for o, dev in enumerate(xpeers):
            g_copy(p, j, X + o, {"row": dev}).start()

    def to_core(p, j):
        g_copy(p, j, CORE, {"row": partner}).start()

    def to_up(p, j):
        @pl.when(l < nd - 1)
        def _():
            g_copy(p, j, UP, {"depth": l + 1}).start()

    def to_down(p, j):
        @pl.when(l > 0)
        def _():
            g_copy(p, j, DOWN, {"depth": l - 1}).start()

    def a_up(q, i):
        @pl.when(l < nd - 1)
        def _():
            a_copy(q, i, UP, {"depth": l + 1}).start()

    def a_down(q, i):
        @pl.when(l > 0)
        def _():
            a_copy(q, i, DOWN, {"depth": l - 1}).start()

    def a_col(q, i):
        for o, dev in enumerate(cpeers):
            a_copy(q, i, 2 + o, {"col": dev}).start()

    def w_copy(j):
        return pltpu.make_async_copy(
            w_ref.at[:, pl.ds(pl.multiple_of(j * cols, cols), cols)], wbuf.at[lax.rem(j, 2)],
            w_sem.at[lax.rem(j, 2)])

    own = l * nr + r
    mine = l * nc + c

    @pl.loop(0, nch)
    def _(j):
        pltpu.make_async_copy(
            g_ref.at[:, pl.ds(pl.multiple_of(j * cols, cols), cols)], piece(own, j), load_sem.at[0]).start()

    own_acts = pltpu.make_async_copy(a_ref, own_a, load_sem.at[1])
    own_acts.start()
    for j in range(min(2, nch)):
        w_copy(j).start()

    barrier = pltpu.get_barrier_semaphore()
    peers = [{"row": partner}] + [{"row": x} for x in xpeers] + [{"col": y} for y in cpeers]
    for dev in peers:
        pl.semaphore_signal(barrier, inc=1, device_id=dev, device_id_type=MESH)

    @pl.when(l > 0)
    def _():
        pl.semaphore_signal(barrier, inc=1, device_id={"depth": l - 1}, device_id_type=MESH)

    @pl.when(l < nd - 1)
    def _():
        pl.semaphore_signal(barrier, inc=1, device_id={"depth": l + 1}, device_id_type=MESH)

    neighbours = jnp.where(l > 0, 1, 0) + jnp.where(l < nd - 1, 1, 0)
    pl.semaphore_wait(barrier, len(peers) + neighbours)
    pltpu.make_async_copy(whole(own), whole(own), load_sem.at[0]).wait()

    to_up(own, 0)
    to_down(own, 0)

    @pl.loop(0, nch)
    def _(j):
        to_x(own, j)

    own_acts.wait()
    acts[:, pl.ds(pl.multiple_of(mine * width, width), width)] = own_a[...].T

    @pl.loop(0, sub)
    def _(i):
        a_up(mine, i)
        a_down(mine, i)
        a_col(mine, i)

    @pl.loop(1, nch)
    def _(j):
        to_up(own, j)
        to_down(own, j)

    @pl.loop(0, nch)
    def _(j):
        to_core(own, j)

    total[...] = jnp.zeros_like(total)

    tile_f = 256

    def tiles(body):
        @pl.loop(0, feats // tile_f)
        def _(i):
            body(pl.ds(pl.multiple_of(i * tile_f, tile_f), tile_f))

    def core_wait(k, j):
        for x in range(nx):
            g_wait(k * nr + x * CORES + 1 - core, j)

    def step(t, carry):
        z = t - 1
        dist = lax.div(z, per) + 1
        v = lax.rem(z, per)
        is_a = (v > 0) & (v <= sub)
        for sign, g_on, a_on in ((-1, to_up, a_up), (1, to_down, a_down)):
            src = l + sign * dist
            there = (z >= 0) & (dist < nd) & (src >= 0) & (src < nd)

            @pl.when(there & ~is_a)
            def _(p=src * nr + r, j=jnp.where(v > 0, v - sub, 0), g_on=g_on):
                g_wait(p, j)
                g_on(p, j)
                to_x(p, j)
                to_core(p, j)

            @pl.when(there & is_a)
            def _(q=src * nc + c, i=v - 1, a_on=a_on):
                a_wait(q, i)
                a_on(q, i)
                a_col(q, i)

        ja = t - late - 2

        @pl.when((ja >= 0) & (ja < nch))
        def _():
            core_wait(l, ja)
            w_copy(ja).wait()
            lhs = grads[ja, pl.ds(pl.multiple_of(l * layer, layer), layer), :]

            def body(at):
                total[:, at] += lax.dot_general(
                    lhs, wbuf[lax.rem(ja, 2), at, :], (((1,), (1,)), ((), ())),
                    preferred_element_type=jnp.float32)

            tiles(body)

            @pl.when(ja + 2 < nch)
            def _():
                w_copy(ja + 2).start()

        @pl.when(ja == nch)
        def _():
            term[...] = total[...].astype(term.dtype)
            for o, dev in enumerate(cpeers):
                pltpu.make_async_remote_copy(
                    src_ref=term.at[pl.ds(pl.multiple_of(dev * block, block), block), :],
                    dst_ref=parts.at[o], send_sem=send_t.at[o], recv_sem=recv_t.at[o],
                    device_id={"col": dev}, device_id_type=MESH).start()

        jb = ja - nch * (nd - 2)

        @pl.when(jb == 0)
        def _():
            for k in range(nd):
                @pl.when(k != last)
                def _(k=k):
                    for dev in cpeers:
                        for i in range(sub):
                            a_wait(k * nc + dev, i)

        @pl.when((jb >= 0) & (jb < nch))
        def _():
            for k in range(nd):
                @pl.when((k != last) & (k != l))
                def _(k=k):
                    core_wait(k, jb)

            tokens = pl.ds(pl.multiple_of(first, layer), (nd - 1) * layer)

            def body(at):
                gw_ref[at, pl.ds(pl.multiple_of(jb * cols, cols), cols)] = jnp.dot(
                    acts[at, tokens], grads[jb, tokens, :], preferred_element_type=jnp.float32).astype(gw_ref.dtype)

            tiles(body)

        jc = jb - nch

        @pl.when(jc == 0)
        def _():
            for dev in cpeers:
                for i in range(sub):
                    a_wait(last * nc + dev, i)

        @pl.when((jc >= 0) & (jc < nch))
        def _():
            core_wait(last, jc)
            tokens = pl.ds(pl.multiple_of(last * layer, layer), layer)

            def body(at):
                here = pl.ds(pl.multiple_of(jc * cols, cols), cols)
                gw_ref[at, here] = (gw_ref[at, here].astype(jnp.float32) + jnp.dot(
                    acts[at, tokens], grads[jc, tokens, :], preferred_element_type=jnp.float32)).astype(gw_ref.dtype)

            tiles(body)

        u = t - late
        e = u - nch
        paired = e < 2 * nch * pairs
        e2 = e - 2 * nch * pairs
        dist = jnp.where(paired, lax.div(e, 2 * nch), pairs + lax.div(e2, nch)) + 1
        j = jnp.where(paired, lax.div(lax.rem(e, 2 * nch), 2), lax.rem(e2, nch))
        up = jnp.where(paired, lax.rem(e, 2) == 1, far_up)
        src = jnp.where(e < 0, l, jnp.where(up, l + dist, l - dist))
        j = jnp.where(e < 0, u, j)

        @pl.when((u >= 0) & (u < nch * nd))
        def _():
            for x in xpeers:
                g_wait(src * nr + x, j)
                to_core(src * nr + x, j)

        return carry

    lax.fori_loop(0, nch * nd + late + 2, step, 0)

    result = total[pl.ds(pl.multiple_of(c * block, block), block), :]
    for o, dev in enumerate(cpeers):
        pltpu.make_async_copy(parts.at[o], parts.at[o], recv_t.at[o]).wait()
        result = result + parts[o].astype(jnp.float32)
    ga_ref[...] = result.astype(ga_ref.dtype)

    for o, dev in enumerate(cpeers):
        pltpu.make_async_copy(parts.at[o], parts.at[o], send_t.at[o]).wait()

    def sent_g(way, p):
        pltpu.make_async_copy(whole(p), whole(p), send_g.at[way, p]).wait()

    def sent_a(way, q):
        pltpu.make_async_copy(awhole(q), awhole(q), send_a.at[way, q]).wait()

    for k in range(nd):
        p, q = k * nr + r, k * nc + c

        @pl.when((k <= l) & (l < nd - 1))
        def _(p=p, q=q):
            sent_g(UP, p)
            sent_a(UP, q)

        @pl.when((k >= l) & (l > 0))
        def _(p=p, q=q):
            sent_g(DOWN, p)
            sent_a(DOWN, q)

        for o in range(len(xpeers)):
            sent_g(X + o, p)
        for x in range(nx):
            sent_g(CORE, k * nr + x * CORES + core)
        for o in range(len(cpeers)):
            sent_a(2 + o, q)


def store(ga_ref, gw_ref, ga_out, gw_out, sem):
    copies = [pltpu.make_async_copy(ga_ref, ga_out, sem.at[0]),
              pltpu.make_async_copy(gw_ref, gw_out, sem.at[1])]
    for copy in copies:
        copy.start()
    for copy in copies:
        copy.wait()


def shards(nd, nr, nc, acts, grad_out, weight):
    rows, width = grad_out.shape
    cols = 512 if width % 512 == 0 else 256
    nch = width // cols
    feats = acts.shape[1]
    layer = nr * rows
    block = layer // nc
    bf16, dma = jnp.bfloat16, pltpu.SemaphoreType.DMA
    anywhere = pl.BlockSpec(memory_space=pl.ANY)
    vmem = pl.BlockSpec(memory_space=pltpu.VMEM)
    nx = nr // CORES
    pieces, apieces = nd * nr, nd * nc
    sub = max(1, acts.size // (rows * cols))
    ga, gw = pl.pallas_call(
        functools.partial(kernel, nd, nr, nc, nch, cols, sub),
        out_shape=(pltpu.VMEM((block, feats), bf16), pltpu.VMEM((feats, width), bf16)),
        in_specs=[anywhere] * 3,
        out_specs=(vmem, vmem),
        scratch_shapes=[
            pltpu.VMEM((nch, pieces * rows, cols), bf16),
            pltpu.VMEM((feats, apieces * acts.shape[0]), bf16),
            pltpu.VMEM(acts.shape, bf16),
            pltpu.VMEM((layer, feats), jnp.float32),
            pltpu.VMEM((layer, feats), bf16),
            pltpu.VMEM((nc - 1, block, feats), bf16),
            pltpu.VMEM((2, feats, cols), bf16),
            dma((pieces, nch)), dma((apieces, sub)), dma((nc - 1,)),
            dma((3 + nx - 1, pieces)), dma((2 + nc - 1, apieces)), dma((nc - 1,)),
            dma((2,)), dma((2,)),
        ],
        compiler_params=pltpu.CompilerParams(
            collective_id=0, has_side_effects=True, vmem_limit_bytes=46 << 20),
    )(acts, grad_out, weight)
    return pl.pallas_call(
        store,
        out_shape=(jax.ShapeDtypeStruct(ga.shape, bf16), jax.ShapeDtypeStruct(gw.shape, bf16)),
        in_specs=[vmem, vmem],
        out_specs=(anywhere, anywhere),
        scratch_shapes=[dma((2,))],
        compiler_params=pltpu.CompilerParams(vmem_limit_bytes=1 << 20),
    )(ga, gw)


def solution(mesh):
    nd, nr, nc = mesh.shape["depth"], mesh.shape["row"], mesh.shape["col"]
    in_specs = (P(("depth", "col"), "row"), P(("depth", "row"), "col"), P("row", "col"))
    out_specs = (P(("depth", "col"), "row"), P("row", "col"))
    return jax.shard_map(functools.partial(shards, nd, nr, nc), mesh=mesh,
                         in_specs=in_specs, out_specs=out_specs, check_vma=False)
```

```python
import functools

import jax
import jax.numpy as jnp
from jax import lax
from jax.experimental import pallas as pl
from jax.experimental.pallas import tpu as pltpu
from jax.sharding import PartitionSpec as P

MESH = pl.DeviceIdType.MESH
CORES = 2

LEAD = 2
TAIL = 3
TILE = 256


def order(nch, spare):
    return [(i + spare) % nch for i in range(nch)]


def lag(nd, nch, sub, spare):
    per = nch + sub
    need = [per * (d - 1) + sub + 1 - nch * d for d in range(1, nd)]
    need += [need[-1] + spare, per * (nd - 2) + sub + LEAD - nch * (nd - 1) - 2]
    return max(0, 1 + max(need))


def kernel(nd, nr, nc, nch, cols, sub, spare, a_ref, g_ref, w_ref, ga_ref, gw_ref, rest_g, rest_a,
           grads, acts, own_a, total, term, parts, wbuf,
           recv_g, recv_h, recv_a, recv_t, send_g, send_a, send_t, load_sem, w_sem):
    nx = nr // CORES
    l, r, c = lax.axis_index("depth"), lax.axis_index("row"), lax.axis_index("col")
    core = lax.rem(r, CORES)
    xi = lax.div(r, CORES)
    partner = xi * CORES + (1 - core)
    xpeers = [lax.rem(xi + o, nx) * CORES + core for o in range(1, nx)]
    cpeers = [lax.rem(c + o, nc) for o in range(1, nc)]
    rows = g_ref.shape[0]
    width, feats = a_ref.shape
    layer = nr * rows
    block = layer // nc
    fsub = feats // sub
    per = nch + sub
    late = lag(nd, nch, sub, spare)
    pairs = jnp.minimum(l, nd - 1 - l)
    far_up = l < nd // 2
    last = jnp.where(far_up, nd - 1, 0)
    first = jnp.where(far_up, 0, layer)
    ends = nch * (nd - 1)
    UP, DOWN, CORE, X = 0, 1, 2, 3

    def piece(p, j):
        return grads.at[j, pl.ds(pl.multiple_of(p * rows, rows), rows), :]

    def whole(p):
        return grads.at[:, pl.ds(pl.multiple_of(p * rows, rows), rows), :]

    def apiece(q, i):
        return acts.at[pl.ds(pl.multiple_of(i * fsub, fsub), fsub), pl.ds(pl.multiple_of(q * width, width), width)]

    def awhole(q):
        return acts.at[:, pl.ds(pl.multiple_of(q * width, width), width)]

    def g_copy(p, j, way, dev):
        return pltpu.make_async_remote_copy(
            src_ref=piece(p, j), dst_ref=piece(p, j), send_sem=send_g.at[way, p],
            recv_sem=recv_g.at[p, j], device_id=dev, device_id_type=MESH)

    def half(p, h):
        return grads.at[nch - 1, pl.ds(pl.multiple_of(p * rows + h * (rows // 2), rows // 2), rows // 2), :]

    def half_copy(p, h, way, sem, dev):
        return pltpu.make_async_remote_copy(
            src_ref=half(p, h), dst_ref=half(p, h), send_sem=send_g.at[way, p],
            recv_sem=sem, device_id=dev, device_id_type=MESH)

    def a_copy(q, i, way, dev):
        return pltpu.make_async_remote_copy(
            src_ref=apiece(q, i), dst_ref=apiece(q, i), send_sem=send_a.at[way, q],
            recv_sem=recv_a.at[q, i], device_id=dev, device_id_type=MESH)

    def g_wait(p, j):
        pltpu.make_async_copy(piece(p, j), piece(p, j), recv_g.at[p, j]).wait()

    def a_wait(q, i):
        pltpu.make_async_copy(apiece(q, i), apiece(q, i), recv_a.at[q, i]).wait()

    def to_x(p, j):
        for o, dev in enumerate(xpeers):
            g_copy(p, j, X + o, {"row": dev}).start()

    def to_core(p, j):
        g_copy(p, j, CORE, {"row": partner}).start()

    def to_up(p, j):
        @pl.when(l < nd - 1)
        def _():
            g_copy(p, j, UP, {"depth": l + 1}).start()

    def to_down(p, j):
        @pl.when(l > 0)
        def _():
            g_copy(p, j, DOWN, {"depth": l - 1}).start()

    def a_up(q, i):
        @pl.when(l < nd - 1)
        def _():
            a_copy(q, i, UP, {"depth": l + 1}).start()

    def a_down(q, i):
        @pl.when(l > 0)
        def _():
            a_copy(q, i, DOWN, {"depth": l - 1}).start()

    def a_col(q, i):
        for o, dev in enumerate(cpeers):
            a_copy(q, i, 2 + o, {"col": dev}).start()

    def w_copy(j):
        return pltpu.make_async_copy(
            w_ref.at[:, pl.ds(pl.multiple_of(j * cols, cols), cols)], wbuf.at[lax.rem(j, 2)],
            w_sem.at[lax.rem(j, 2)])

    own = l * nr + r
    mine = l * nc + c

    def from_own(j):
        src = g_ref.at[:, pl.ds(pl.multiple_of(j * cols, cols), cols)]

        def send(way, dev):
            pltpu.make_async_remote_copy(
                src_ref=src, dst_ref=piece(own, j), send_sem=send_g.at[way, own],
                recv_sem=recv_g.at[own, j], device_id=dev, device_id_type=MESH).start()

        @pl.when(l < nd - 1)
        def _():
            send(UP, {"depth": l + 1})

        @pl.when(l > 0)
        def _():
            send(DOWN, {"depth": l - 1})

        for o, dev in enumerate(xpeers):
            send(X + o, {"row": dev})

    barrier = pltpu.get_barrier_semaphore()
    peers = [{"row": partner}] + [{"row": x} for x in xpeers] + [{"col": y} for y in cpeers]
    for dev in peers:
        pl.semaphore_signal(barrier, inc=1, device_id=dev, device_id_type=MESH)

    @pl.when(l > 0)
    def _():
        pl.semaphore_signal(barrier, inc=1, device_id={"depth": l - 1}, device_id_type=MESH)

    @pl.when(l < nd - 1)
    def _():
        pl.semaphore_signal(barrier, inc=1, device_id={"depth": l + 1}, device_id_type=MESH)

    @pl.loop(0, nch)
    def _(j):
        pltpu.make_async_copy(
            g_ref.at[:, pl.ds(pl.multiple_of(j * cols, cols), cols)], piece(own, j), load_sem.at[j]).start()

    own_acts = pltpu.make_async_copy(a_ref, own_a, load_sem.at[nch])
    own_acts.start()

    neighbours = jnp.where(l > 0, 1, 0) + jnp.where(l < nd - 1, 1, 0)
    pl.semaphore_wait(barrier, len(peers) + neighbours)

    for j in range(LEAD):
        from_own(j)

    own_acts.wait()
    acts[:, pl.ds(pl.multiple_of(mine * width, width), width)] = own_a[...].T

    @pl.loop(0, sub)
    def _(i):
        a_up(mine, i)
        a_down(mine, i)
        a_col(mine, i)

    @pl.loop(LEAD, nch)
    def _(j):
        from_own(j)

    @pl.loop(0, nch)
    def _(j):
        pltpu.make_async_copy(piece(own, j), piece(own, j), load_sem.at[j]).wait()
        to_core(own, j)

    for j in range(min(2, nch)):
        w_copy(j).start()

    total[...] = jnp.zeros_like(total)

    def tiles(body):
        @pl.loop(0, feats // TILE)
        def _(i):
            body(pl.ds(pl.multiple_of(i * TILE, TILE), TILE))

    def core_wait(k, j):
        for x in range(nx):
            g_wait(k * nr + x * CORES + 1 - core, j)

    def sent_g(way, p):
        pltpu.make_async_copy(whole(p), whole(p), send_g.at[way, p]).wait()

    def sent_one(way, p):
        pltpu.make_async_copy(piece(p, 0), piece(p, 0), send_g.at[way, p]).wait()

    def sent_a(way, q):
        pltpu.make_async_copy(awhole(q), awhole(q), send_a.at[way, q]).wait()

    def sent(k, pieces):
        p, q = k * nr + r, k * nc + c

        @pl.when((k <= l) & (l < nd - 1))
        def _():
            sent_g(UP, p)
            sent_a(UP, q)

        @pl.when((k >= l) & (l > 0))
        def _():
            sent_g(DOWN, p)
            sent_a(DOWN, q)

        part = grads.at[pl.ds(0, pieces), pl.ds(pl.multiple_of(p * rows, rows), rows), :]
        for o in range(len(xpeers)):
            pltpu.make_async_copy(part, part, send_g.at[X + o, p]).wait()
        for x in range(nx):
            sent_g(CORE, k * nr + x * CORES + core)
        for o in range(len(cpeers)):
            sent_a(2 + o, q)

    def step(t, carry):
        z = t - 1
        dist = lax.div(z, per) + 1
        v = lax.rem(z, per)
        is_a = (v >= LEAD) & (v < LEAD + sub)
        for sign, g_on, a_on in ((-1, to_up, a_up), (1, to_down, a_down)):
            src = l + sign * dist
            there = (z >= 0) & (dist < nd) & (src >= 0) & (src < nd)

            @pl.when(there & ~is_a)
            def _(p=src * nr + r, j=jnp.where(v < LEAD, v, v - sub), g_on=g_on, src=src, sign=sign):
                if spare:
                    final = (src == last) & (j == nch - 1)
                    halved = final & ((l == 0) | (l == nd - 1))
                    halves = final & ((l == nd - 2) if sign < 0 else (l == 1))

                    @pl.when(halved)
                    def _():
                        for h in range(2):
                            pltpu.make_async_copy(half(p, h), half(p, h), recv_h.at[h]).wait()
                            half_copy(p, h, X, recv_g.at[p, nch - 1], {"row": xpeers[0]}).start()

                    @pl.when(halves)
                    def _():
                        g_wait(p, j)
                        for h in range(2):
                            if sign < 0:
                                half_copy(p, h, UP, recv_h.at[h], {"depth": l + 1}).start()
                            else:
                                half_copy(p, h, DOWN, recv_h.at[h], {"depth": l - 1}).start()

                    @pl.when(~halved & ~halves)
                    def _():
                        g_wait(p, j)
                        g_on(p, j)

                    @pl.when(((src != last) | (j > 0)) & ~halved)
                    def _():
                        to_x(p, j)
                else:
                    g_wait(p, j)
                    g_on(p, j)
                    to_x(p, j)
                to_core(p, j)

            @pl.when(there & is_a)
            def _(q=src * nc + c, i=v - LEAD, a_on=a_on):
                a_wait(q, i)
                a_on(q, i)
                a_col(q, i)

        if spare:
            p = last * nr + xpeers[0]

            @pl.when((t == per * (nd - 1 - l) + 1) & far_up)
            def _():
                g_wait(p, 0)
                to_down(p, 0)
                to_core(p, 0)

            @pl.when((t == per * l + 1) & ~far_up)
            def _():
                g_wait(p, 0)
                to_up(p, 0)
                to_core(p, 0)

            @pl.when((t == per * (nd // 2 - 1) + 1) & (l == nd // 2))
            def _():
                to_down((nd - 1) * nr + xpeers[0], 0)

            @pl.when((t == per * (nd // 2 - 1) + 1) & (l == nd // 2 - 1))
            def _():
                to_up(xpeers[0], 0)

        ja = t - late - 2

        @pl.when((ja >= 0) & (ja < nch))
        def _():
            core_wait(l, ja)
            w_copy(ja).wait()
            lhs = grads[ja, pl.ds(pl.multiple_of(l * layer, layer), layer), :]

            def body(at):
                total[:, at] += lax.dot_general(
                    lhs, wbuf[lax.rem(ja, 2), at, :], (((1,), (1,)), ((), ())),
                    preferred_element_type=jnp.float32)

            tiles(body)

            @pl.when(ja + 2 < nch)
            def _():
                w_copy(ja + 2).start()

        @pl.when(ja == nch)
        def _():
            term[...] = total[...].astype(term.dtype)
            for o, dev in enumerate(cpeers):
                pltpu.make_async_remote_copy(
                    src_ref=term.at[pl.ds(pl.multiple_of(dev * block, block), block), :],
                    dst_ref=parts.at[o], send_sem=send_t.at[o], recv_sem=recv_t.at[o],
                    device_id={"col": dev}, device_id_type=MESH).start()

        @pl.when(ja == nch + 8)
        def _():
            result = total[pl.ds(pl.multiple_of(c * block, block), block), :]
            for o in range(len(cpeers)):
                pltpu.make_async_copy(parts.at[o], parts.at[o], recv_t.at[o]).wait()
                result = result + parts[o].astype(jnp.float32)
            ga_ref[...] = result.astype(ga_ref.dtype)
            for o in range(len(cpeers)):
                pltpu.make_async_copy(parts.at[o], parts.at[o], send_t.at[o]).wait()

        jb = ja - nch * (nd - 2)

        @pl.when(jb == 0)
        def _():
            for k in range(nd):
                @pl.when(k != last)
                def _(k=k):
                    for dev in cpeers:
                        for i in range(sub):
                            a_wait(k * nc + dev, i)

        @pl.when((jb >= 0) & (jb < nch))
        def _():
            for k in range(nd):
                @pl.when((k != last) & (k != l))
                def _(k=k):
                    core_wait(k, jb)

            tokens = pl.ds(pl.multiple_of(first, layer), (nd - 1) * layer)

            def body(at):
                gw_ref[at, pl.ds(pl.multiple_of(jb * cols, cols), cols)] = jnp.dot(
                    acts[at, tokens], grads[jb, tokens, :], preferred_element_type=jnp.float32).astype(gw_ref.dtype)

            tiles(body)

        jc = jb - nch

        @pl.when(jc == 4)
        def _():
            rest_a[...] = acts[:, pl.ds(pl.multiple_of(last * layer, layer), layer)]
            for k in range(nd):
                @pl.when(k != last)
                def _(k=k):
                    sent(k, nch)

        @pl.when(jc == 0)
        def _():
            for dev in cpeers:
                for i in range(sub):
                    a_wait(last * nc + dev, i)

        @pl.when((jc >= 0) & (jc < nch - TAIL))
        def _():
            j = lax.rem(jc + spare, nch)
            core_wait(last, j)
            tokens = pl.ds(pl.multiple_of(last * layer, layer), layer)

            def body(at):
                here = pl.ds(pl.multiple_of(j * cols, cols), cols)
                gw_ref[at, here] = (gw_ref[at, here].astype(jnp.float32) + jnp.dot(
                    acts[at, tokens], grads[j, tokens, :], preferred_element_type=jnp.float32)).astype(gw_ref.dtype)

            tiles(body)

        @pl.when((jc >= nch - TAIL) & (jc < nch - 2))
        def _():
            j = lax.rem(jc + spare, nch)
            core_wait(last, j)
            rest_g[jc - (nch - TAIL)] = grads[j, pl.ds(pl.multiple_of(last * layer, layer), layer), :]

        u = t - late
        if spare:
            u = jnp.where(u >= ends, u + 1, u)
        e = u - nch
        paired = e < 2 * nch * pairs
        e2 = e - 2 * nch * pairs
        dist = jnp.where(paired, lax.div(e, 2 * nch), pairs + lax.div(e2, nch)) + 1
        j = jnp.where(paired, lax.div(lax.rem(e, 2 * nch), 2), lax.rem(e2, nch))
        up = jnp.where(paired, lax.rem(e, 2) == 1, far_up)
        src = jnp.where(e < 0, l, jnp.where(up, l + dist, l - dist))
        j = jnp.where(e < 0, u, j)

        @pl.when((u >= 0) & (u < nch * nd))
        def _():
            for x in xpeers:
                g_wait(src * nr + x, j)
                to_core(src * nr + x, j)

        return carry

    lax.fori_loop(0, nch * nd + late, step, 0)
    for i, j in list(enumerate(order(nch, spare)[nch - TAIL:]))[-2:]:
        core_wait(last, j)
        rest_g[i] = grads[j, pl.ds(pl.multiple_of(last * layer, layer), layer), :]

    sent(last, nch - spare)

    if spare:
        p = last * nr + xpeers[0]

        @pl.when((l > 0) & far_up)
        def _():
            sent_one(DOWN, p)

        @pl.when((l < nd - 1) & ~far_up)
        def _():
            sent_one(UP, p)

        @pl.when(l == nd // 2)
        def _():
            sent_one(DOWN, (nd - 1) * nr + xpeers[0])

        @pl.when(l == nd // 2 - 1)
        def _():
            sent_one(UP, xpeers[0])


def store(nch, spare, ga_ref, gw_ref, rest_g, rest_a, ga_out, gw_out, rest, sem):
    feats, cols = gw_ref.shape[0], rest_g.shape[2]
    done = [j for i, j in enumerate(order(nch, spare)) if i < nch - TAIL]
    whole = pl.ds(min(done) * cols, len(done) * cols)
    copies = [pltpu.make_async_copy(gw_ref.at[:, whole], gw_out.at[:, whole], sem.at[TAIL]),
              pltpu.make_async_copy(ga_ref, ga_out, sem.at[TAIL + 1])]
    for copy in copies:
        copy.start()
    for i, j in enumerate(order(nch, spare)[nch - TAIL:]):
        here = pl.ds(j * cols, cols)

        @pl.loop(0, feats // TILE)
        def _(k):
            f = pl.ds(pl.multiple_of(k * TILE, TILE), TILE)
            rest[i, f, :] = (gw_ref[f, here].astype(jnp.float32) + jnp.dot(
                rest_a[f, :], rest_g[i], preferred_element_type=jnp.float32)).astype(rest.dtype)

        copies.append(pltpu.make_async_copy(rest.at[i], gw_out.at[:, here], sem.at[i]))
        copies[-1].start()
    for copy in copies:
        copy.wait()


def shards(nd, nr, nc, acts, grad_out, weight):
    rows, width = grad_out.shape
    cols = 512 if width % 512 == 0 else 256
    nch = width // cols
    feats = acts.shape[1]
    layer = nr * rows
    block = layer // nc
    bf16, dma = jnp.bfloat16, pltpu.SemaphoreType.DMA
    anywhere = pl.BlockSpec(memory_space=pl.ANY)
    vmem = pl.BlockSpec(memory_space=pltpu.VMEM)
    nx = nr // CORES
    pieces, apieces = nd * nr, nd * nc
    sub = max(1, acts.size // (rows * cols))
    spare = int(nx == 2 and nd > 2 and
                nch * (nd - 3) + 1 + lag(nd, nch, sub, 1) < (nch + sub) * (nd // 2 - 1) + 1)
    ga, gw, rest_g, rest_a = pl.pallas_call(
        functools.partial(kernel, nd, nr, nc, nch, cols, sub, spare),
        out_shape=(
            pltpu.VMEM((block, feats), bf16),
            pltpu.VMEM((feats, width), bf16),
            pltpu.VMEM((TAIL, layer, cols), bf16),
            pltpu.VMEM((feats, layer), bf16),
        ),
        in_specs=[anywhere] * 3,
        out_specs=(vmem,) * 4,
        scratch_shapes=[
            pltpu.VMEM((nch, pieces * rows, cols), bf16),
            pltpu.VMEM((feats, apieces * acts.shape[0]), bf16),
            pltpu.VMEM(acts.shape, bf16),
            pltpu.VMEM((layer, feats), jnp.float32),
            pltpu.VMEM((layer, feats), bf16),
            pltpu.VMEM((nc - 1, block, feats), bf16),
            pltpu.VMEM((2, feats, cols), bf16),
            dma((pieces, nch)), dma((2,)), dma((apieces, sub)), dma((nc - 1,)),
            dma((3 + nx - 1, pieces)), dma((2 + nc - 1, apieces)), dma((nc - 1,)),
            dma((nch + 1,)), dma((2,)),
        ],
        compiler_params=pltpu.CompilerParams(
            collective_id=0, has_side_effects=True, vmem_limit_bytes=43 << 20),
    )(acts, grad_out, weight)
    return pl.pallas_call(
        functools.partial(store, nch, spare),
        out_shape=(jax.ShapeDtypeStruct(ga.shape, bf16), jax.ShapeDtypeStruct(gw.shape, bf16)),
        in_specs=[vmem] * 4,
        out_specs=(anywhere, anywhere),
        scratch_shapes=[pltpu.VMEM((TAIL, feats, cols), bf16), dma((TAIL + 2,))],
        compiler_params=pltpu.CompilerParams(vmem_limit_bytes=6 << 20),
    )(ga, gw, rest_g, rest_a)


def solution(mesh):
    nd, nr, nc = mesh.shape["depth"], mesh.shape["row"], mesh.shape["col"]
    in_specs = (P(("depth", "col"), "row"), P(("depth", "row"), "col"), P("row", "col"))
    out_specs = (P(("depth", "col"), "row"), P("row", "col"))
    return jax.shard_map(functools.partial(shards, nd, nr, nc), mesh=mesh,
                         in_specs=in_specs, out_specs=out_specs, check_vma=False)
```

```python
import functools

import jax
import jax.numpy as jnp
from jax import lax
from jax.experimental import pallas as pl
from jax.experimental.pallas import tpu as pltpu
from jax.sharding import PartitionSpec as P

MESH = pl.DeviceIdType.MESH
CORES = 2

LEAD = 2
TAIL = 3
TILE = 256


def order(nch, spare):
    return [(i + spare) % nch for i in range(nch)]


def lag(nd, nch, sub, spare):
    per = nch + sub
    need = [per * (d - 1) + sub + 1 - nch * d for d in range(1, nd)]
    need += [need[-1] + spare, per * (nd - 2) + sub + LEAD - nch * (nd - 1) - 2]
    return max(0, 1 + max(need))


def kernel(nd, nr, nc, nch, cols, sub, spare, a_ref, g_ref, w_ref, ga_ref, gw_ref, rest_g, rest_a,
           grads, acts, own_a, total, term, parts, wbuf,
           recv_g, recv_a, recv_t, send_g, send_a, send_t, load_sem, w_sem):
    nx = nr // CORES
    l, r, c = lax.axis_index("depth"), lax.axis_index("row"), lax.axis_index("col")
    core = lax.rem(r, CORES)
    xi = lax.div(r, CORES)
    partner = xi * CORES + (1 - core)
    xpeers = [lax.rem(xi + o, nx) * CORES + core for o in range(1, nx)]
    cpeers = [lax.rem(c + o, nc) for o in range(1, nc)]
    rows = g_ref.shape[0]
    width, feats = a_ref.shape
    layer = nr * rows
    block = layer // nc
    fsub = feats // sub
    per = nch + sub
    late = lag(nd, nch, sub, spare)
    pairs = jnp.minimum(l, nd - 1 - l)
    far_up = l < nd // 2
    last = jnp.where(far_up, nd - 1, 0)
    first = jnp.where(far_up, 0, layer)
    ends = nch * (nd - 1)
    UP, DOWN, CORE, X = 0, 1, 2, 3

    def piece(p, j):
        return grads.at[j, pl.ds(pl.multiple_of(p * rows, rows), rows), :]

    def whole(p):
        return grads.at[:, pl.ds(pl.multiple_of(p * rows, rows), rows), :]

    def apiece(q, i):
        return acts.at[pl.ds(pl.multiple_of(i * fsub, fsub), fsub), pl.ds(pl.multiple_of(q * width, width), width)]

    def awhole(q):
        return acts.at[:, pl.ds(pl.multiple_of(q * width, width), width)]

    def g_copy(p, j, way, dev):
        return pltpu.make_async_remote_copy(
            src_ref=piece(p, j), dst_ref=piece(p, j), send_sem=send_g.at[way, p],
            recv_sem=recv_g.at[p, j], device_id=dev, device_id_type=MESH)

    def a_copy(q, i, way, dev):
        return pltpu.make_async_remote_copy(
            src_ref=apiece(q, i), dst_ref=apiece(q, i), send_sem=send_a.at[way, q],
            recv_sem=recv_a.at[q, i], device_id=dev, device_id_type=MESH)

    def g_wait(p, j):
        pltpu.make_async_copy(piece(p, j), piece(p, j), recv_g.at[p, j]).wait()

    def a_wait(q, i):
        pltpu.make_async_copy(apiece(q, i), apiece(q, i), recv_a.at[q, i]).wait()

    def to_x(p, j):
        for o, dev in enumerate(xpeers):
            g_copy(p, j, X + o, {"row": dev}).start()

    def to_core(p, j):
        g_copy(p, j, CORE, {"row": partner}).start()

    def to_up(p, j):
        @pl.when(l < nd - 1)
        def _():
            g_copy(p, j, UP, {"depth": l + 1}).start()

    def to_down(p, j):
        @pl.when(l > 0)
        def _():
            g_copy(p, j, DOWN, {"depth": l - 1}).start()

    def a_up(q, i):
        @pl.when(l < nd - 1)
        def _():
            a_copy(q, i, UP, {"depth": l + 1}).start()

    def a_down(q, i):
        @pl.when(l > 0)
        def _():
            a_copy(q, i, DOWN, {"depth": l - 1}).start()

    def a_col(q, i):
        for o, dev in enumerate(cpeers):
            a_copy(q, i, 2 + o, {"col": dev}).start()

    def w_copy(j):
        return pltpu.make_async_copy(
            w_ref.at[:, pl.ds(pl.multiple_of(j * cols, cols), cols)], wbuf.at[lax.rem(j, 2)],
            w_sem.at[lax.rem(j, 2)])

    own = l * nr + r
    mine = l * nc + c

    def from_own(j):
        src = g_ref.at[:, pl.ds(pl.multiple_of(j * cols, cols), cols)]

        def send(way, dev):
            pltpu.make_async_remote_copy(
                src_ref=src, dst_ref=piece(own, j), send_sem=send_g.at[way, own],
                recv_sem=recv_g.at[own, j], device_id=dev, device_id_type=MESH).start()

        @pl.when(l < nd - 1)
        def _():
            send(UP, {"depth": l + 1})

        @pl.when(l > 0)
        def _():
            send(DOWN, {"depth": l - 1})

        for o, dev in enumerate(xpeers):
            send(X + o, {"row": dev})

    barrier = pltpu.get_barrier_semaphore()
    peers = [{"row": partner}] + [{"row": x} for x in xpeers] + [{"col": y} for y in cpeers]
    for dev in peers:
        pl.semaphore_signal(barrier, inc=1, device_id=dev, device_id_type=MESH)

    @pl.when(l > 0)
    def _():
        pl.semaphore_signal(barrier, inc=1, device_id={"depth": l - 1}, device_id_type=MESH)

    @pl.when(l < nd - 1)
    def _():
        pl.semaphore_signal(barrier, inc=1, device_id={"depth": l + 1}, device_id_type=MESH)

    @pl.loop(0, nch)
    def _(j):
        pltpu.make_async_copy(
            g_ref.at[:, pl.ds(pl.multiple_of(j * cols, cols), cols)], piece(own, j), load_sem.at[j]).start()

    own_acts = pltpu.make_async_copy(a_ref, own_a, load_sem.at[nch])
    own_acts.start()

    neighbours = jnp.where(l > 0, 1, 0) + jnp.where(l < nd - 1, 1, 0)
    pl.semaphore_wait(barrier, len(peers) + neighbours)

    for j in range(LEAD):
        from_own(j)

    own_acts.wait()
    acts[:, pl.ds(pl.multiple_of(mine * width, width), width)] = own_a[...].T

    @pl.loop(0, sub)
    def _(i):
        a_up(mine, i)
        a_down(mine, i)
        a_col(mine, i)

    @pl.loop(LEAD, nch)
    def _(j):
        from_own(j)

    @pl.loop(0, nch)
    def _(j):
        pltpu.make_async_copy(piece(own, j), piece(own, j), load_sem.at[j]).wait()
        to_core(own, j)

    for j in range(min(2, nch)):
        w_copy(j).start()

    total[...] = jnp.zeros_like(total)

    def tiles(body):
        @pl.loop(0, feats // TILE)
        def _(i):
            body(pl.ds(pl.multiple_of(i * TILE, TILE), TILE))

    def core_wait(k, j):
        for x in range(nx):
            g_wait(k * nr + x * CORES + 1 - core, j)

    def sent_g(way, p):
        pltpu.make_async_copy(whole(p), whole(p), send_g.at[way, p]).wait()

    def sent_one(way, p):
        pltpu.make_async_copy(piece(p, 0), piece(p, 0), send_g.at[way, p]).wait()

    def sent_a(way, q):
        pltpu.make_async_copy(awhole(q), awhole(q), send_a.at[way, q]).wait()

    def sent(k, pieces):
        p, q = k * nr + r, k * nc + c

        @pl.when((k <= l) & (l < nd - 1))
        def _():
            sent_g(UP, p)
            sent_a(UP, q)

        @pl.when((k >= l) & (l > 0))
        def _():
            sent_g(DOWN, p)
            sent_a(DOWN, q)

        part = grads.at[pl.ds(0, pieces), pl.ds(pl.multiple_of(p * rows, rows), rows), :]
        for o in range(len(xpeers)):
            pltpu.make_async_copy(part, part, send_g.at[X + o, p]).wait()
        for x in range(nx):
            sent_g(CORE, k * nr + x * CORES + core)
        for o in range(len(cpeers)):
            sent_a(2 + o, q)

    def step(t, carry):
        z = t - 1
        dist = lax.div(z, per) + 1
        v = lax.rem(z, per)
        turn = jnp.where((dist == nd - 1) & (nd > 2), spare, 0)
        lead = LEAD - turn
        is_a = (v >= lead) & (v < lead + sub)
        jz = jnp.where(v < lead, v, v - sub) + turn
        jz = jnp.where(jz < nch, jz, 0)
        for sign, g_on, a_on in ((-1, to_up, a_up), (1, to_down, a_down)):
            src = l + sign * dist
            there = (z >= 0) & (dist < nd) & (src >= 0) & (src < nd)

            @pl.when(there & ~is_a)
            def _(p=src * nr + r, g_on=g_on, src=src, sign=sign):
                g_wait(p, jz)
                if spare:
                    kept = (src == last) & (jz == 0)

                    @pl.when(~(kept & ((l == nd - 2) if sign < 0 else (l == 1))))
                    def _():
                        g_on(p, jz)

                    @pl.when(~kept)
                    def _():
                        to_x(p, jz)
                else:
                    g_on(p, jz)
                    to_x(p, jz)
                to_core(p, jz)

            @pl.when(there & is_a)
            def _(q=src * nc + c, i=v - lead, a_on=a_on):
                a_wait(q, i)
                a_on(q, i)
                a_col(q, i)

        if spare:
            p = last * nr + xpeers[0]

            @pl.when((t == per * (nd - 1 - l) + 1) & far_up)
            def _():
                @pl.when(l == 1)
                def _():
                    to_down(last * nr + r, 0)

                g_wait(p, 0)
                to_down(p, 0)
                to_core(p, 0)

            @pl.when((t == per * l + 1) & ~far_up)
            def _():
                @pl.when(l == nd - 2)
                def _():
                    to_up(last * nr + r, 0)

                g_wait(p, 0)
                to_up(p, 0)
                to_core(p, 0)

            @pl.when((t == per * (nd // 2 - 1) + 1) & (l == nd // 2))
            def _():
                to_down((nd - 1) * nr + xpeers[0], 0)

            @pl.when((t == per * (nd // 2 - 1) + 1) & (l == nd // 2 - 1))
            def _():
                to_up(xpeers[0], 0)

        ja = t - late - 2

        @pl.when((ja >= 0) & (ja < nch))
        def _():
            core_wait(l, ja)
            w_copy(ja).wait()
            lhs = grads[ja, pl.ds(pl.multiple_of(l * layer, layer), layer), :]

            def body(at):
                total[:, at] += lax.dot_general(
                    lhs, wbuf[lax.rem(ja, 2), at, :], (((1,), (1,)), ((), ())),
                    preferred_element_type=jnp.float32)

            tiles(body)

            @pl.when(ja + 2 < nch)
            def _():
                w_copy(ja + 2).start()

        @pl.when(ja == nch)
        def _():
            term[...] = total[...].astype(term.dtype)
            for o, dev in enumerate(cpeers):
                pltpu.make_async_remote_copy(
                    src_ref=term.at[pl.ds(pl.multiple_of(dev * block, block), block), :],
                    dst_ref=parts.at[o], send_sem=send_t.at[o], recv_sem=recv_t.at[o],
                    device_id={"col": dev}, device_id_type=MESH).start()

        @pl.when(ja == nch + 8)
        def _():
            result = total[pl.ds(pl.multiple_of(c * block, block), block), :]
            for o in range(len(cpeers)):
                pltpu.make_async_copy(parts.at[o], parts.at[o], recv_t.at[o]).wait()
                result = result + parts[o].astype(jnp.float32)
            ga_ref[...] = result.astype(ga_ref.dtype)
            for o in range(len(cpeers)):
                pltpu.make_async_copy(parts.at[o], parts.at[o], send_t.at[o]).wait()

        jb = ja - nch * (nd - 2)

        @pl.when(jb == 0)
        def _():
            for k in range(nd):
                @pl.when(k != last)
                def _(k=k):
                    for dev in cpeers:
                        for i in range(sub):
                            a_wait(k * nc + dev, i)

        @pl.when((jb >= 0) & (jb < nch))
        def _():
            for k in range(nd):
                @pl.when((k != last) & (k != l))
                def _(k=k):
                    core_wait(k, jb)

            tokens = pl.ds(pl.multiple_of(first, layer), (nd - 1) * layer)

            def body(at):
                gw_ref[at, pl.ds(pl.multiple_of(jb * cols, cols), cols)] = jnp.dot(
                    acts[at, tokens], grads[jb, tokens, :], preferred_element_type=jnp.float32).astype(gw_ref.dtype)

            tiles(body)

        jc = jb - nch

        @pl.when(jc == 4)
        def _():
            rest_a[...] = acts[:, pl.ds(pl.multiple_of(last * layer, layer), layer)]
            for k in range(nd):
                @pl.when(k != last)
                def _(k=k):
                    sent(k, nch)

        @pl.when(jc == 0)
        def _():
            for dev in cpeers:
                for i in range(sub):
                    a_wait(last * nc + dev, i)

        @pl.when((jc >= 0) & (jc < nch - TAIL))
        def _():
            j = lax.rem(jc + spare, nch)
            core_wait(last, j)
            tokens = pl.ds(pl.multiple_of(last * layer, layer), layer)

            def body(at):
                here = pl.ds(pl.multiple_of(j * cols, cols), cols)
                gw_ref[at, here] = (gw_ref[at, here].astype(jnp.float32) + jnp.dot(
                    acts[at, tokens], grads[j, tokens, :], preferred_element_type=jnp.float32)).astype(gw_ref.dtype)

            tiles(body)

        @pl.when((jc >= nch - TAIL) & (jc < nch - 2))
        def _():
            j = lax.rem(jc + spare, nch)
            core_wait(last, j)
            rest_g[jc - (nch - TAIL)] = grads[j, pl.ds(pl.multiple_of(last * layer, layer), layer), :]

        u = t - late
        if spare:
            u = jnp.where(u >= ends, u + 1, u)
        e = u - nch
        paired = e < 2 * nch * pairs
        e2 = e - 2 * nch * pairs
        dist = jnp.where(paired, lax.div(e, 2 * nch), pairs + lax.div(e2, nch)) + 1
        j = jnp.where(paired, lax.div(lax.rem(e, 2 * nch), 2), lax.rem(e2, nch))
        up = jnp.where(paired, lax.rem(e, 2) == 1, far_up)
        src = jnp.where(e < 0, l, jnp.where(up, l + dist, l - dist))
        j = jnp.where(e < 0, u, j)

        @pl.when((u >= 0) & (u < nch * nd))
        def _():
            for x in xpeers:
                g_wait(src * nr + x, j)
                to_core(src * nr + x, j)

        return carry

    lax.fori_loop(0, nch * nd + late, step, 0)
    for i, j in list(enumerate(order(nch, spare)[nch - TAIL:]))[-2:]:
        core_wait(last, j)
        rest_g[i] = grads[j, pl.ds(pl.multiple_of(last * layer, layer), layer), :]

    sent(last, nch - spare)

    if spare:
        p = last * nr + xpeers[0]

        @pl.when((l > 0) & far_up)
        def _():
            sent_one(DOWN, p)

        @pl.when((l < nd - 1) & ~far_up)
        def _():
            sent_one(UP, p)

        @pl.when(l == nd // 2)
        def _():
            sent_one(DOWN, (nd - 1) * nr + xpeers[0])

        @pl.when(l == nd // 2 - 1)
        def _():
            sent_one(UP, xpeers[0])


def store(nch, spare, ga_ref, gw_ref, rest_g, rest_a, ga_out, gw_out, rest, sem):
    feats, cols = gw_ref.shape[0], rest_g.shape[2]
    done = [j for i, j in enumerate(order(nch, spare)) if i < nch - TAIL]
    whole = pl.ds(min(done) * cols, len(done) * cols)
    copies = [pltpu.make_async_copy(gw_ref.at[:, whole], gw_out.at[:, whole], sem.at[TAIL]),
              pltpu.make_async_copy(ga_ref, ga_out, sem.at[TAIL + 1])]
    for copy in copies:
        copy.start()
    for i, j in enumerate(order(nch, spare)[nch - TAIL:]):
        here = pl.ds(j * cols, cols)

        @pl.loop(0, feats // TILE)
        def _(k):
            f = pl.ds(pl.multiple_of(k * TILE, TILE), TILE)
            rest[i, f, :] = (gw_ref[f, here].astype(jnp.float32) + jnp.dot(
                rest_a[f, :], rest_g[i], preferred_element_type=jnp.float32)).astype(rest.dtype)

        copies.append(pltpu.make_async_copy(rest.at[i], gw_out.at[:, here], sem.at[i]))
        copies[-1].start()
    for copy in copies:
        copy.wait()


def shards(nd, nr, nc, acts, grad_out, weight):
    rows, width = grad_out.shape
    cols = 512 if width % 512 == 0 else 256
    nch = width // cols
    feats = acts.shape[1]
    layer = nr * rows
    block = layer // nc
    bf16, dma = jnp.bfloat16, pltpu.SemaphoreType.DMA
    anywhere = pl.BlockSpec(memory_space=pl.ANY)
    vmem = pl.BlockSpec(memory_space=pltpu.VMEM)
    nx = nr // CORES
    pieces, apieces = nd * nr, nd * nc
    sub = max(1, acts.size // (rows * cols))
    spare = int(nx == 2 and nd > 2 and
                nch * (nd - 3) + 1 + lag(nd, nch, sub, 1) < (nch + sub) * (nd // 2 - 1) + 1)
    ga, gw, rest_g, rest_a = pl.pallas_call(
        functools.partial(kernel, nd, nr, nc, nch, cols, sub, spare),
        out_shape=(
            pltpu.VMEM((block, feats), bf16),
            pltpu.VMEM((feats, width), bf16),
            pltpu.VMEM((TAIL, layer, cols), bf16),
            pltpu.VMEM((feats, layer), bf16),
        ),
        in_specs=[anywhere] * 3,
        out_specs=(vmem,) * 4,
        scratch_shapes=[
            pltpu.VMEM((nch, pieces * rows, cols), bf16),
            pltpu.VMEM((feats, apieces * acts.shape[0]), bf16),
            pltpu.VMEM(acts.shape, bf16),
            pltpu.VMEM((layer, feats), jnp.float32),
            pltpu.VMEM((layer, feats), bf16),
            pltpu.VMEM((nc - 1, block, feats), bf16),
            pltpu.VMEM((2, feats, cols), bf16),
            dma((pieces, nch)), dma((apieces, sub)), dma((nc - 1,)),
            dma((3 + nx - 1, pieces)), dma((2 + nc - 1, apieces)), dma((nc - 1,)),
            dma((nch + 1,)), dma((2,)),
        ],
        compiler_params=pltpu.CompilerParams(
            collective_id=0, has_side_effects=True, vmem_limit_bytes=43 << 20),
    )(acts, grad_out, weight)
    return pl.pallas_call(
        functools.partial(store, nch, spare),
        out_shape=(jax.ShapeDtypeStruct(ga.shape, bf16), jax.ShapeDtypeStruct(gw.shape, bf16)),
        in_specs=[vmem] * 4,
        out_specs=(anywhere, anywhere),
        scratch_shapes=[pltpu.VMEM((TAIL, feats, cols), bf16), dma((TAIL + 2,))],
        compiler_params=pltpu.CompilerParams(vmem_limit_bytes=6 << 20),
    )(ga, gw, rest_g, rest_a)


def solution(mesh):
    nd, nr, nc = mesh.shape["depth"], mesh.shape["row"], mesh.shape["col"]
    in_specs = (P(("depth", "col"), "row"), P(("depth", "row"), "col"), P("row", "col"))
    out_specs = (P(("depth", "col"), "row"), P("row", "col"))
    return jax.shard_map(functools.partial(shards, nd, nr, nc), mesh=mesh,
                         in_specs=in_specs, out_specs=out_specs, check_vma=False)
```

```python
import functools

import jax
import jax.numpy as jnp
from jax import lax
from jax.experimental import pallas as pl
from jax.experimental.pallas import tpu as pltpu
from jax.sharding import PartitionSpec as P

MESH = pl.DeviceIdType.MESH
CORES = 2

LEAD = 2
TAIL = 3
TILE = 256


def order(nch, spare):
    return [(i + spare) % nch for i in range(nch)]


def lag(nd, nch, sub):
    per = nch + sub
    need = [per * (d - 1) + sub + 1 - nch * d for d in range(1, nd)]
    need += [per * (nd - 2) + sub + LEAD - nch * (nd - 1) - 2]
    return max(0, 1 + max(need))


def kernel(nd, nr, nc, nch, cols, sub, spare, a_ref, g_ref, w_ref, ga_ref, gw_ref, rest_g, rest_a,
           grads, acts, own_a, total, term, parts, wbuf,
           recv_g, recv_a, recv_t, send_g, send_a, send_t, load_sem, w_sem):
    nx = nr // CORES
    l, r, c = lax.axis_index("depth"), lax.axis_index("row"), lax.axis_index("col")
    core = lax.rem(r, CORES)
    xi = lax.div(r, CORES)
    partner = xi * CORES + (1 - core)
    xpeers = [lax.rem(xi + o, nx) * CORES + core for o in range(1, nx)]
    cpeers = [lax.rem(c + o, nc) for o in range(1, nc)]
    rows = g_ref.shape[0]
    width, feats = a_ref.shape
    layer = nr * rows
    block = layer // nc
    fsub = feats // sub
    per = nch + sub
    late = lag(nd, nch, sub)
    pairs = jnp.minimum(l, nd - 1 - l)
    far_up = l < nd // 2
    last = jnp.where(far_up, nd - 1, 0)
    first = jnp.where(far_up, 0, layer)
    ends = nch * (nd - 1)
    UP, DOWN, CORE, X = 0, 1, 2, 3

    def piece(p, j):
        return grads.at[j, pl.ds(pl.multiple_of(p * rows, rows), rows), :]

    def whole(p):
        return grads.at[:, pl.ds(pl.multiple_of(p * rows, rows), rows), :]

    def apiece(q, i):
        return acts.at[pl.ds(pl.multiple_of(i * fsub, fsub), fsub), pl.ds(pl.multiple_of(q * width, width), width)]

    def awhole(q):
        return acts.at[:, pl.ds(pl.multiple_of(q * width, width), width)]

    def g_copy(p, j, way, dev):
        return pltpu.make_async_remote_copy(
            src_ref=piece(p, j), dst_ref=piece(p, j), send_sem=send_g.at[way, p],
            recv_sem=recv_g.at[p, j], device_id=dev, device_id_type=MESH)

    def a_copy(q, i, way, dev):
        return pltpu.make_async_remote_copy(
            src_ref=apiece(q, i), dst_ref=apiece(q, i), send_sem=send_a.at[way, q],
            recv_sem=recv_a.at[q, i], device_id=dev, device_id_type=MESH)

    def g_wait(p, j):
        pltpu.make_async_copy(piece(p, j), piece(p, j), recv_g.at[p, j]).wait()

    def a_wait(q, i):
        pltpu.make_async_copy(apiece(q, i), apiece(q, i), recv_a.at[q, i]).wait()

    def to_x(p, j):
        for o, dev in enumerate(xpeers):
            g_copy(p, j, X + o, {"row": dev}).start()

    def to_core(p, j):
        g_copy(p, j, CORE, {"row": partner}).start()

    def to_up(p, j):
        @pl.when(l < nd - 1)
        def _():
            g_copy(p, j, UP, {"depth": l + 1}).start()

    def to_down(p, j):
        @pl.when(l > 0)
        def _():
            g_copy(p, j, DOWN, {"depth": l - 1}).start()

    def a_up(q, i):
        @pl.when(l < nd - 1)
        def _():
            a_copy(q, i, UP, {"depth": l + 1}).start()

    def a_down(q, i):
        @pl.when(l > 0)
        def _():
            a_copy(q, i, DOWN, {"depth": l - 1}).start()

    def a_col(q, i):
        for o, dev in enumerate(cpeers):
            a_copy(q, i, 2 + o, {"col": dev}).start()

    def w_copy(j):
        return pltpu.make_async_copy(
            w_ref.at[:, pl.ds(pl.multiple_of(j * cols, cols), cols)], wbuf.at[lax.rem(j, 2)],
            w_sem.at[lax.rem(j, 2)])

    own = l * nr + r
    mine = l * nc + c

    def from_own(j):
        src = g_ref.at[:, pl.ds(pl.multiple_of(j * cols, cols), cols)]

        def send(way, dev):
            pltpu.make_async_remote_copy(
                src_ref=src, dst_ref=piece(own, j), send_sem=send_g.at[way, own],
                recv_sem=recv_g.at[own, j], device_id=dev, device_id_type=MESH).start()

        @pl.when(l < nd - 1)
        def _():
            send(UP, {"depth": l + 1})

        @pl.when(l > 0)
        def _():
            send(DOWN, {"depth": l - 1})

        for o, dev in enumerate(xpeers):
            send(X + o, {"row": dev})

    barrier = pltpu.get_barrier_semaphore()
    peers = [{"row": partner}] + [{"row": x} for x in xpeers] + [{"col": y} for y in cpeers]
    for dev in peers:
        pl.semaphore_signal(barrier, inc=1, device_id=dev, device_id_type=MESH)

    @pl.when(l > 0)
    def _():
        pl.semaphore_signal(barrier, inc=1, device_id={"depth": l - 1}, device_id_type=MESH)

    @pl.when(l < nd - 1)
    def _():
        pl.semaphore_signal(barrier, inc=1, device_id={"depth": l + 1}, device_id_type=MESH)

    @pl.loop(0, nch)
    def _(j):
        pltpu.make_async_copy(
            g_ref.at[:, pl.ds(pl.multiple_of(j * cols, cols), cols)], piece(own, j), load_sem.at[j]).start()

    own_acts = pltpu.make_async_copy(a_ref, own_a, load_sem.at[nch])
    own_acts.start()

    neighbours = jnp.where(l > 0, 1, 0) + jnp.where(l < nd - 1, 1, 0)
    pl.semaphore_wait(barrier, len(peers) + neighbours)

    for j in range(LEAD):
        from_own(j)

    own_acts.wait()
    acts[:, pl.ds(pl.multiple_of(mine * width, width), width)] = own_a[...].T

    @pl.loop(0, sub)
    def _(i):
        a_up(mine, i)
        a_down(mine, i)
        a_col(mine, i)

    @pl.loop(LEAD, nch)
    def _(j):
        from_own(j)

    @pl.loop(0, nch)
    def _(j):
        pltpu.make_async_copy(piece(own, j), piece(own, j), load_sem.at[j]).wait()
        to_core(own, j)

    for j in range(min(2, nch)):
        w_copy(j).start()

    total[...] = jnp.zeros_like(total)

    def tiles(body):
        @pl.loop(0, feats // TILE)
        def _(i):
            body(pl.ds(pl.multiple_of(i * TILE, TILE), TILE))

    def core_wait(k, j):
        for x in range(nx):
            g_wait(k * nr + x * CORES + 1 - core, j)

    def sent_g(way, p):
        pltpu.make_async_copy(whole(p), whole(p), send_g.at[way, p]).wait()

    def sent_one(way, p):
        pltpu.make_async_copy(piece(p, 0), piece(p, 0), send_g.at[way, p]).wait()

    def sent_a(way, q):
        pltpu.make_async_copy(awhole(q), awhole(q), send_a.at[way, q]).wait()

    def sent(k, pieces):
        p, q = k * nr + r, k * nc + c

        @pl.when((k <= l) & (l < nd - 1))
        def _():
            sent_g(UP, p)
            sent_a(UP, q)

        @pl.when((k >= l) & (l > 0))
        def _():
            sent_g(DOWN, p)
            sent_a(DOWN, q)

        part = grads.at[pl.ds(0, pieces), pl.ds(pl.multiple_of(p * rows, rows), rows), :]
        for o in range(len(xpeers)):
            pltpu.make_async_copy(part, part, send_g.at[X + o, p]).wait()
        for x in range(nx):
            sent_g(CORE, k * nr + x * CORES + core)
        for o in range(len(cpeers)):
            sent_a(2 + o, q)

    def step(t, carry):
        z = t - 1
        dist = lax.div(z, per) + 1
        v = lax.rem(z, per)
        turn = jnp.where((dist == nd - 1) & (nd > 2), spare, 0)
        lead = LEAD - turn
        is_a = (v >= lead) & (v < lead + sub)
        jz = jnp.where(v < lead, v, v - sub) + turn
        jz = jnp.where(jz < nch, jz, 0)
        for sign, g_on, a_on in ((-1, to_up, a_up), (1, to_down, a_down)):
            src = l + sign * dist
            there = (z >= 0) & (dist < nd) & (src >= 0) & (src < nd)

            @pl.when(there & ~is_a)
            def _(p=src * nr + r, g_on=g_on, src=src, sign=sign):
                g_wait(p, jz)
                if spare:
                    kept = (src == last) & (jz == 0)

                    @pl.when(~(kept & ((l == nd - 2) if sign < 0 else (l == 1))))
                    def _():
                        g_on(p, jz)

                    @pl.when(~kept)
                    def _():
                        to_x(p, jz)
                else:
                    g_on(p, jz)
                    to_x(p, jz)
                to_core(p, jz)

            @pl.when(there & is_a)
            def _(q=src * nc + c, i=v - lead, a_on=a_on):
                a_wait(q, i)
                a_on(q, i)
                a_col(q, i)

        if spare:
            p = last * nr + xpeers[0]

            @pl.when((t == per * (nd - 1 - l) + 1) & far_up)
            def _():
                @pl.when(l == 1)
                def _():
                    to_down(last * nr + r, 0)

                g_wait(p, 0)
                to_down(p, 0)
                to_core(p, 0)

            @pl.when((t == per * l + 1) & ~far_up)
            def _():
                @pl.when(l == nd - 2)
                def _():
                    to_up(last * nr + r, 0)

                g_wait(p, 0)
                to_up(p, 0)
                to_core(p, 0)

            @pl.when((t == per * (nd // 2 - 1) + 1) & (l == nd // 2))
            def _():
                to_down((nd - 1) * nr + xpeers[0], 0)

            @pl.when((t == per * (nd // 2 - 1) + 1) & (l == nd // 2 - 1))
            def _():
                to_up(xpeers[0], 0)

        ja = t - late - 2

        @pl.when((ja >= 0) & (ja < nch))
        def _():
            core_wait(l, ja)
            w_copy(ja).wait()
            lhs = grads[ja, pl.ds(pl.multiple_of(l * layer, layer), layer), :]

            def body(at):
                total[:, at] += lax.dot_general(
                    lhs, wbuf[lax.rem(ja, 2), at, :], (((1,), (1,)), ((), ())),
                    preferred_element_type=jnp.float32)

            tiles(body)

            @pl.when(ja + 2 < nch)
            def _():
                w_copy(ja + 2).start()

        @pl.when(ja == nch)
        def _():
            term[...] = total[...].astype(term.dtype)
            for o, dev in enumerate(cpeers):
                pltpu.make_async_remote_copy(
                    src_ref=term.at[pl.ds(pl.multiple_of(dev * block, block), block), :],
                    dst_ref=parts.at[o], send_sem=send_t.at[o], recv_sem=recv_t.at[o],
                    device_id={"col": dev}, device_id_type=MESH).start()

        @pl.when(ja == nch + 8)
        def _():
            result = total[pl.ds(pl.multiple_of(c * block, block), block), :]
            for o in range(len(cpeers)):
                pltpu.make_async_copy(parts.at[o], parts.at[o], recv_t.at[o]).wait()
                result = result + parts[o].astype(jnp.float32)
            ga_ref[...] = result.astype(ga_ref.dtype)
            for o in range(len(cpeers)):
                pltpu.make_async_copy(parts.at[o], parts.at[o], send_t.at[o]).wait()

        jb = ja - nch * (nd - 2)

        @pl.when(jb == 0)
        def _():
            for k in range(nd):
                @pl.when(k != last)
                def _(k=k):
                    for dev in cpeers:
                        for i in range(sub):
                            a_wait(k * nc + dev, i)

        @pl.when((jb >= 0) & (jb < nch))
        def _():
            for k in range(nd):
                @pl.when((k != last) & (k != l))
                def _(k=k):
                    core_wait(k, jb)

            tokens = pl.ds(pl.multiple_of(first, layer), (nd - 1) * layer)

            def body(at):
                gw_ref[at, pl.ds(pl.multiple_of(jb * cols, cols), cols)] = jnp.dot(
                    acts[at, tokens], grads[jb, tokens, :], preferred_element_type=jnp.float32).astype(gw_ref.dtype)

            tiles(body)

        jc = jb - nch

        @pl.when(jc == 4)
        def _():
            rest_a[...] = acts[:, pl.ds(pl.multiple_of(last * layer, layer), layer)]
            for k in range(nd):
                @pl.when(k != last)
                def _(k=k):
                    sent(k, nch)

        @pl.when(jc == 0)
        def _():
            for dev in cpeers:
                for i in range(sub):
                    a_wait(last * nc + dev, i)

        @pl.when((jc >= 0) & (jc < nch - TAIL))
        def _():
            j = lax.rem(jc + spare, nch)
            core_wait(last, j)
            tokens = pl.ds(pl.multiple_of(last * layer, layer), layer)

            def body(at):
                here = pl.ds(pl.multiple_of(j * cols, cols), cols)
                gw_ref[at, here] = (gw_ref[at, here].astype(jnp.float32) + jnp.dot(
                    acts[at, tokens], grads[j, tokens, :], preferred_element_type=jnp.float32)).astype(gw_ref.dtype)

            tiles(body)

        @pl.when((jc >= nch - TAIL) & (jc < nch - 2))
        def _():
            j = lax.rem(jc + spare, nch)
            core_wait(last, j)
            rest_g[jc - (nch - TAIL)] = grads[j, pl.ds(pl.multiple_of(last * layer, layer), layer), :]

        u = t - late
        if spare:
            u = jnp.where(u >= ends, u + 1, u)
        e = u - nch
        paired = e < 2 * nch * pairs
        e2 = e - 2 * nch * pairs
        dist = jnp.where(paired, lax.div(e, 2 * nch), pairs + lax.div(e2, nch)) + 1
        j = jnp.where(paired, lax.div(lax.rem(e, 2 * nch), 2), lax.rem(e2, nch))
        up = jnp.where(paired, lax.rem(e, 2) == 1, far_up)
        src = jnp.where(e < 0, l, jnp.where(up, l + dist, l - dist))
        j = jnp.where(e < 0, u, j)

        @pl.when((u >= 0) & (u < nch * nd))
        def _():
            for x in xpeers:
                g_wait(src * nr + x, j)
                to_core(src * nr + x, j)

        return carry

    lax.fori_loop(0, nch * nd + late, step, 0)
    for i, j in list(enumerate(order(nch, spare)[nch - TAIL:]))[-2:]:
        core_wait(last, j)
        rest_g[i] = grads[j, pl.ds(pl.multiple_of(last * layer, layer), layer), :]

    sent(last, nch - spare)

    if spare:
        p = last * nr + xpeers[0]

        @pl.when((l > 0) & far_up)
        def _():
            sent_one(DOWN, p)

        @pl.when((l < nd - 1) & ~far_up)
        def _():
            sent_one(UP, p)

        @pl.when(l == nd // 2)
        def _():
            sent_one(DOWN, (nd - 1) * nr + xpeers[0])

        @pl.when(l == nd // 2 - 1)
        def _():
            sent_one(UP, xpeers[0])


def store(nch, spare, ga_ref, gw_ref, rest_g, rest_a, ga_out, gw_out, rest, sem):
    feats, cols = gw_ref.shape[0], rest_g.shape[2]
    done = [j for i, j in enumerate(order(nch, spare)) if i < nch - TAIL]
    whole = pl.ds(min(done) * cols, len(done) * cols)
    copies = [pltpu.make_async_copy(gw_ref.at[:, whole], gw_out.at[:, whole], sem.at[TAIL]),
              pltpu.make_async_copy(ga_ref, ga_out, sem.at[TAIL + 1])]
    for copy in copies:
        copy.start()
    for i, j in enumerate(order(nch, spare)[nch - TAIL:]):
        here = pl.ds(j * cols, cols)

        @pl.loop(0, feats // TILE)
        def _(k):
            f = pl.ds(pl.multiple_of(k * TILE, TILE), TILE)
            rest[i, f, :] = (gw_ref[f, here].astype(jnp.float32) + jnp.dot(
                rest_a[f, :], rest_g[i], preferred_element_type=jnp.float32)).astype(rest.dtype)

        copies.append(pltpu.make_async_copy(rest.at[i], gw_out.at[:, here], sem.at[i]))
        copies[-1].start()
    for copy in copies:
        copy.wait()


def shards(nd, nr, nc, acts, grad_out, weight):
    rows, width = grad_out.shape
    cols = 512 if width % 512 == 0 else 256
    nch = width // cols
    feats = acts.shape[1]
    layer = nr * rows
    block = layer // nc
    bf16, dma = jnp.bfloat16, pltpu.SemaphoreType.DMA
    anywhere = pl.BlockSpec(memory_space=pl.ANY)
    vmem = pl.BlockSpec(memory_space=pltpu.VMEM)
    nx = nr // CORES
    pieces, apieces = nd * nr, nd * nc
    sub = max(1, acts.size // (rows * cols))
    spare = int(nx == 2 and nd > 2 and
                nch * (nd - 3) + 1 + lag(nd, nch, sub) < (nch + sub) * (nd // 2 - 1) + 1)
    ga, gw, rest_g, rest_a = pl.pallas_call(
        functools.partial(kernel, nd, nr, nc, nch, cols, sub, spare),
        out_shape=(
            pltpu.VMEM((block, feats), bf16),
            pltpu.VMEM((feats, width), bf16),
            pltpu.VMEM((TAIL, layer, cols), bf16),
            pltpu.VMEM((feats, layer), bf16),
        ),
        in_specs=[anywhere] * 3,
        out_specs=(vmem,) * 4,
        scratch_shapes=[
            pltpu.VMEM((nch, pieces * rows, cols), bf16),
            pltpu.VMEM((feats, apieces * acts.shape[0]), bf16),
            pltpu.VMEM(acts.shape, bf16),
            pltpu.VMEM((layer, feats), jnp.float32),
            pltpu.VMEM((layer, feats), bf16),
            pltpu.VMEM((nc - 1, block, feats), bf16),
            pltpu.VMEM((2, feats, cols), bf16),
            dma((pieces, nch)), dma((apieces, sub)), dma((nc - 1,)),
            dma((3 + nx - 1, pieces)), dma((2 + nc - 1, apieces)), dma((nc - 1,)),
            dma((nch + 1,)), dma((2,)),
        ],
        compiler_params=pltpu.CompilerParams(
            collective_id=0, has_side_effects=True, vmem_limit_bytes=43 << 20),
    )(acts, grad_out, weight)
    return pl.pallas_call(
        functools.partial(store, nch, spare),
        out_shape=(jax.ShapeDtypeStruct(ga.shape, bf16), jax.ShapeDtypeStruct(gw.shape, bf16)),
        in_specs=[vmem] * 4,
        out_specs=(anywhere, anywhere),
        scratch_shapes=[pltpu.VMEM((TAIL, feats, cols), bf16), dma((TAIL + 2,))],
        compiler_params=pltpu.CompilerParams(vmem_limit_bytes=6 << 20),
    )(ga, gw, rest_g, rest_a)


def solution(mesh):
    nd, nr, nc = mesh.shape["depth"], mesh.shape["row"], mesh.shape["col"]
    in_specs = (P(("depth", "col"), "row"), P(("depth", "row"), "col"), P("row", "col"))
    out_specs = (P(("depth", "col"), "row"), P("row", "col"))
    return jax.shard_map(functools.partial(shards, nd, nr, nc), mesh=mesh,
                         in_specs=in_specs, out_specs=out_specs, check_vma=False)
```

```python
import functools

import jax
import jax.numpy as jnp
from jax import lax
from jax.experimental import pallas as pl
from jax.experimental.pallas import tpu as pltpu
from jax.sharding import PartitionSpec as P

MESH = pl.DeviceIdType.MESH
CORES = 2

LEAD = 2
TAIL = 3
STORES = 8
TILE = 256


def order(nch, spare):
    return [(i + spare) % nch for i in range(nch)]


def lag(nd, nch, sub):
    per = nch + sub
    need = [per * (d - 1) + sub + 1 - nch * d for d in range(1, nd)]
    need += [per * (nd - 2) + sub + LEAD - nch * (nd - 1) - 2]
    return max(0, 1 + max(need))


def kernel(nd, nr, nc, nch, cols, sub, spare, a_ref, g_ref, w_ref, ga_ref, gw_ref, rest_g, rest_a,
           grads, acts, own_a, total, term, parts, wbuf,
           recv_g, recv_a, recv_t, send_g, send_a, send_t, load_sem, w_sem):
    nx = nr // CORES
    l, r, c = lax.axis_index("depth"), lax.axis_index("row"), lax.axis_index("col")
    core = lax.rem(r, CORES)
    xi = lax.div(r, CORES)
    partner = xi * CORES + (1 - core)
    xpeers = [lax.rem(xi + o, nx) * CORES + core for o in range(1, nx)]
    cpeers = [lax.rem(c + o, nc) for o in range(1, nc)]
    rows = g_ref.shape[0]
    width, feats = a_ref.shape
    layer = nr * rows
    block = layer // nc
    fsub = feats // sub
    per = nch + sub
    late = lag(nd, nch, sub)
    pairs = jnp.minimum(l, nd - 1 - l)
    far_up = l < nd // 2
    last = jnp.where(far_up, nd - 1, 0)
    first = jnp.where(far_up, 0, layer)
    ends = nch * (nd - 1)
    UP, DOWN, CORE, X = 0, 1, 2, 3

    def piece(p, j):
        return grads.at[j, pl.ds(pl.multiple_of(p * rows, rows), rows), :]

    def whole(p):
        return grads.at[:, pl.ds(pl.multiple_of(p * rows, rows), rows), :]

    def apiece(q, i):
        return acts.at[pl.ds(pl.multiple_of(i * fsub, fsub), fsub), pl.ds(pl.multiple_of(q * width, width), width)]

    def awhole(q):
        return acts.at[:, pl.ds(pl.multiple_of(q * width, width), width)]

    def g_copy(p, j, way, dev):
        return pltpu.make_async_remote_copy(
            src_ref=piece(p, j), dst_ref=piece(p, j), send_sem=send_g.at[way, p],
            recv_sem=recv_g.at[p, j], device_id=dev, device_id_type=MESH)

    def a_copy(q, i, way, dev):
        return pltpu.make_async_remote_copy(
            src_ref=apiece(q, i), dst_ref=apiece(q, i), send_sem=send_a.at[way, q],
            recv_sem=recv_a.at[q, i], device_id=dev, device_id_type=MESH)

    def g_wait(p, j):
        pltpu.make_async_copy(piece(p, j), piece(p, j), recv_g.at[p, j]).wait()

    def a_wait(q, i):
        pltpu.make_async_copy(apiece(q, i), apiece(q, i), recv_a.at[q, i]).wait()

    def to_x(p, j):
        for o, dev in enumerate(xpeers):
            g_copy(p, j, X + o, {"row": dev}).start()

    def to_core(p, j):
        g_copy(p, j, CORE, {"row": partner}).start()

    def to_up(p, j):
        @pl.when(l < nd - 1)
        def _():
            g_copy(p, j, UP, {"depth": l + 1}).start()

    def to_down(p, j):
        @pl.when(l > 0)
        def _():
            g_copy(p, j, DOWN, {"depth": l - 1}).start()

    def a_up(q, i):
        @pl.when(l < nd - 1)
        def _():
            a_copy(q, i, UP, {"depth": l + 1}).start()

    def a_down(q, i):
        @pl.when(l > 0)
        def _():
            a_copy(q, i, DOWN, {"depth": l - 1}).start()

    def a_col(q, i):
        for o, dev in enumerate(cpeers):
            a_copy(q, i, 2 + o, {"col": dev}).start()

    def w_copy(j):
        return pltpu.make_async_copy(
            w_ref.at[:, pl.ds(pl.multiple_of(j * cols, cols), cols)], wbuf.at[lax.rem(j, 2)],
            w_sem.at[lax.rem(j, 2)])

    own = l * nr + r
    mine = l * nc + c

    def from_own(j):
        src = g_ref.at[:, pl.ds(pl.multiple_of(j * cols, cols), cols)]

        def send(way, dev):
            pltpu.make_async_remote_copy(
                src_ref=src, dst_ref=piece(own, j), send_sem=send_g.at[way, own],
                recv_sem=recv_g.at[own, j], device_id=dev, device_id_type=MESH).start()

        @pl.when(l < nd - 1)
        def _():
            send(UP, {"depth": l + 1})

        @pl.when(l > 0)
        def _():
            send(DOWN, {"depth": l - 1})

        for o, dev in enumerate(xpeers):
            send(X + o, {"row": dev})

    barrier = pltpu.get_barrier_semaphore()
    peers = [{"row": partner}] + [{"row": x} for x in xpeers] + [{"col": y} for y in cpeers]
    for dev in peers:
        pl.semaphore_signal(barrier, inc=1, device_id=dev, device_id_type=MESH)

    @pl.when(l > 0)
    def _():
        pl.semaphore_signal(barrier, inc=1, device_id={"depth": l - 1}, device_id_type=MESH)

    @pl.when(l < nd - 1)
    def _():
        pl.semaphore_signal(barrier, inc=1, device_id={"depth": l + 1}, device_id_type=MESH)

    @pl.loop(0, nch)
    def _(j):
        pltpu.make_async_copy(
            g_ref.at[:, pl.ds(pl.multiple_of(j * cols, cols), cols)], piece(own, j), load_sem.at[j]).start()

    own_acts = pltpu.make_async_copy(a_ref, own_a, load_sem.at[nch])
    own_acts.start()

    neighbours = jnp.where(l > 0, 1, 0) + jnp.where(l < nd - 1, 1, 0)
    pl.semaphore_wait(barrier, len(peers) + neighbours)

    for j in range(LEAD):
        from_own(j)

    own_acts.wait()
    acts[:, pl.ds(pl.multiple_of(mine * width, width), width)] = own_a[...].T

    @pl.loop(0, sub)
    def _(i):
        a_up(mine, i)
        a_down(mine, i)
        a_col(mine, i)

    @pl.loop(LEAD, nch)
    def _(j):
        from_own(j)

    @pl.loop(0, nch)
    def _(j):
        pltpu.make_async_copy(piece(own, j), piece(own, j), load_sem.at[j]).wait()
        to_core(own, j)

    for j in range(min(2, nch)):
        w_copy(j).start()

    total[...] = jnp.zeros_like(total)

    def tiles(body):
        @pl.loop(0, feats // TILE)
        def _(i):
            body(pl.ds(pl.multiple_of(i * TILE, TILE), TILE))

    def core_wait(k, j):
        for x in range(nx):
            g_wait(k * nr + x * CORES + 1 - core, j)

    def sent_g(way, p):
        pltpu.make_async_copy(whole(p), whole(p), send_g.at[way, p]).wait()

    def sent_one(way, p):
        pltpu.make_async_copy(piece(p, 0), piece(p, 0), send_g.at[way, p]).wait()

    def sent_a(way, q):
        pltpu.make_async_copy(awhole(q), awhole(q), send_a.at[way, q]).wait()

    def sent(k, pieces):
        p, q = k * nr + r, k * nc + c

        @pl.when((k <= l) & (l < nd - 1))
        def _():
            sent_g(UP, p)
            sent_a(UP, q)

        @pl.when((k >= l) & (l > 0))
        def _():
            sent_g(DOWN, p)
            sent_a(DOWN, q)

        part = grads.at[pl.ds(0, pieces), pl.ds(pl.multiple_of(p * rows, rows), rows), :]
        for o in range(len(xpeers)):
            pltpu.make_async_copy(part, part, send_g.at[X + o, p]).wait()
        for x in range(nx):
            sent_g(CORE, k * nr + x * CORES + core)
        for o in range(len(cpeers)):
            sent_a(2 + o, q)

    def step(t, carry):
        z = t - 1
        dist = lax.div(z, per) + 1
        v = lax.rem(z, per)
        turn = jnp.where((dist == nd - 1) & (nd > 2), spare, 0)
        lead = LEAD - turn
        is_a = (v >= lead) & (v < lead + sub)
        jz = jnp.where(v < lead, v, v - sub) + turn
        jz = jnp.where(jz < nch, jz, 0)
        for sign, g_on, a_on in ((-1, to_up, a_up), (1, to_down, a_down)):
            src = l + sign * dist
            there = (z >= 0) & (dist < nd) & (src >= 0) & (src < nd)

            @pl.when(there & ~is_a)
            def _(p=src * nr + r, g_on=g_on, src=src, sign=sign):
                g_wait(p, jz)
                if spare:
                    kept = (src == last) & (jz == 0)

                    @pl.when(~(kept & ((l == nd - 2) if sign < 0 else (l == 1))))
                    def _():
                        g_on(p, jz)

                    @pl.when(~kept)
                    def _():
                        to_x(p, jz)
                else:
                    g_on(p, jz)
                    to_x(p, jz)
                to_core(p, jz)

            @pl.when(there & is_a)
            def _(q=src * nc + c, i=v - lead, a_on=a_on):
                a_wait(q, i)
                a_on(q, i)
                a_col(q, i)

        if spare:
            p = last * nr + xpeers[0]

            @pl.when((t == per * (nd - 1 - l) + 1) & far_up)
            def _():
                @pl.when(l == 1)
                def _():
                    to_down(last * nr + r, 0)

                g_wait(p, 0)
                to_down(p, 0)
                to_core(p, 0)

            @pl.when((t == per * l + 1) & ~far_up)
            def _():
                @pl.when(l == nd - 2)
                def _():
                    to_up(last * nr + r, 0)

                g_wait(p, 0)
                to_up(p, 0)
                to_core(p, 0)

            @pl.when((t == per * (nd // 2 - 1) + 1) & (l == nd // 2))
            def _():
                to_down((nd - 1) * nr + xpeers[0], 0)

            @pl.when((t == per * (nd // 2 - 1) + 1) & (l == nd // 2 - 1))
            def _():
                to_up(xpeers[0], 0)

        ja = t - late - 2

        @pl.when((ja >= 0) & (ja < nch))
        def _():
            core_wait(l, ja)
            w_copy(ja).wait()
            lhs = grads[ja, pl.ds(pl.multiple_of(l * layer, layer), layer), :]

            def body(at):
                total[:, at] += lax.dot_general(
                    lhs, wbuf[lax.rem(ja, 2), at, :], (((1,), (1,)), ((), ())),
                    preferred_element_type=jnp.float32)

            tiles(body)

            @pl.when(ja + 2 < nch)
            def _():
                w_copy(ja + 2).start()

        @pl.when(ja == nch)
        def _():
            term[...] = total[...].astype(term.dtype)
            for o, dev in enumerate(cpeers):
                pltpu.make_async_remote_copy(
                    src_ref=term.at[pl.ds(pl.multiple_of(dev * block, block), block), :],
                    dst_ref=parts.at[o], send_sem=send_t.at[o], recv_sem=recv_t.at[o],
                    device_id={"col": dev}, device_id_type=MESH).start()

        @pl.when(ja == nch + 8)
        def _():
            result = total[pl.ds(pl.multiple_of(c * block, block), block), :]
            for o in range(len(cpeers)):
                pltpu.make_async_copy(parts.at[o], parts.at[o], recv_t.at[o]).wait()
                result = result + parts[o].astype(jnp.float32)
            ga_ref[...] = result.astype(ga_ref.dtype)
            for o in range(len(cpeers)):
                pltpu.make_async_copy(parts.at[o], parts.at[o], send_t.at[o]).wait()

        jb = ja - nch * (nd - 2)

        @pl.when(jb == 0)
        def _():
            for k in range(nd):
                @pl.when(k != last)
                def _(k=k):
                    for dev in cpeers:
                        for i in range(sub):
                            a_wait(k * nc + dev, i)

        @pl.when((jb >= 0) & (jb < nch))
        def _():
            for k in range(nd):
                @pl.when((k != last) & (k != l))
                def _(k=k):
                    core_wait(k, jb)

            tokens = pl.ds(pl.multiple_of(first, layer), (nd - 1) * layer)

            def body(at):
                gw_ref[at, pl.ds(pl.multiple_of(jb * cols, cols), cols)] = jnp.dot(
                    acts[at, tokens], grads[jb, tokens, :], preferred_element_type=jnp.float32).astype(gw_ref.dtype)

            tiles(body)

        jc = jb - nch

        @pl.when(jc == 4)
        def _():
            rest_a[...] = acts[:, pl.ds(pl.multiple_of(last * layer, layer), layer)]
            for k in range(nd):
                @pl.when(k != last)
                def _(k=k):
                    sent(k, nch)

        @pl.when(jc == 0)
        def _():
            for dev in cpeers:
                for i in range(sub):
                    a_wait(last * nc + dev, i)

        @pl.when((jc >= 0) & (jc < nch - TAIL))
        def _():
            j = lax.rem(jc + spare, nch)
            core_wait(last, j)
            tokens = pl.ds(pl.multiple_of(last * layer, layer), layer)

            def body(at):
                here = pl.ds(pl.multiple_of(j * cols, cols), cols)
                gw_ref[at, here] = (gw_ref[at, here].astype(jnp.float32) + jnp.dot(
                    acts[at, tokens], grads[j, tokens, :], preferred_element_type=jnp.float32)).astype(gw_ref.dtype)

            tiles(body)

        @pl.when((jc >= nch - TAIL) & (jc < nch - 2))
        def _():
            j = lax.rem(jc + spare, nch)
            core_wait(last, j)
            rest_g[jc - (nch - TAIL)] = grads[j, pl.ds(pl.multiple_of(last * layer, layer), layer), :]

        u = t - late
        if spare:
            u = jnp.where(u >= ends, u + 1, u)
        e = u - nch
        paired = e < 2 * nch * pairs
        e2 = e - 2 * nch * pairs
        dist = jnp.where(paired, lax.div(e, 2 * nch), pairs + lax.div(e2, nch)) + 1
        j = jnp.where(paired, lax.div(lax.rem(e, 2 * nch), 2), lax.rem(e2, nch))
        up = jnp.where(paired, lax.rem(e, 2) == 1, far_up)
        src = jnp.where(e < 0, l, jnp.where(up, l + dist, l - dist))
        j = jnp.where(e < 0, u, j)

        @pl.when((u >= 0) & (u < nch * nd))
        def _():
            for x in xpeers:
                g_wait(src * nr + x, j)
                to_core(src * nr + x, j)

        return carry

    lax.fori_loop(0, nch * nd + late, step, 0)
    for i, j in list(enumerate(order(nch, spare)[nch - TAIL:]))[-2:]:
        core_wait(last, j)
        rest_g[i] = grads[j, pl.ds(pl.multiple_of(last * layer, layer), layer), :]

    sent(last, nch - spare)

    if spare:
        p = last * nr + xpeers[0]

        @pl.when((l > 0) & far_up)
        def _():
            sent_one(DOWN, p)

        @pl.when((l < nd - 1) & ~far_up)
        def _():
            sent_one(UP, p)

        @pl.when(l == nd // 2)
        def _():
            sent_one(DOWN, (nd - 1) * nr + xpeers[0])

        @pl.when(l == nd // 2 - 1)
        def _():
            sent_one(UP, xpeers[0])


def store(nch, spare, ga_ref, gw_ref, rest_g, rest_a, ga_out, gw_out, rest, sem):
    feats, cols = gw_ref.shape[0], rest_g.shape[2]
    done = [j for i, j in enumerate(order(nch, spare)) if i < nch - TAIL]
    whole = pl.ds(min(done) * cols, len(done) * cols)
    copies = [pltpu.make_async_copy(ga_ref, ga_out, sem.at[TAIL + STORES])]
    for i in range(STORES):
        part = pl.ds(i * (feats // STORES), feats // STORES)
        copies.append(pltpu.make_async_copy(gw_ref.at[part, whole], gw_out.at[part, whole], sem.at[TAIL + i]))
    for copy in copies:
        copy.start()
    for i, j in enumerate(order(nch, spare)[nch - TAIL:]):
        here = pl.ds(j * cols, cols)

        @pl.loop(0, feats // TILE)
        def _(k):
            f = pl.ds(pl.multiple_of(k * TILE, TILE), TILE)
            rest[i, f, :] = (gw_ref[f, here].astype(jnp.float32) + jnp.dot(
                rest_a[f, :], rest_g[i], preferred_element_type=jnp.float32)).astype(rest.dtype)

        copies.append(pltpu.make_async_copy(rest.at[i], gw_out.at[:, here], sem.at[i]))
        copies[-1].start()
    for copy in copies:
        copy.wait()


def shards(nd, nr, nc, acts, grad_out, weight):
    rows, width = grad_out.shape
    cols = 512 if width % 512 == 0 else 256
    nch = width // cols
    feats = acts.shape[1]
    layer = nr * rows
    block = layer // nc
    bf16, dma = jnp.bfloat16, pltpu.SemaphoreType.DMA
    anywhere = pl.BlockSpec(memory_space=pl.ANY)
    vmem = pl.BlockSpec(memory_space=pltpu.VMEM)
    nx = nr // CORES
    pieces, apieces = nd * nr, nd * nc
    sub = max(1, acts.size // (rows * cols))
    spare = int(nx == 2 and nd > 2 and
                nch * (nd - 3) + 1 + lag(nd, nch, sub) < (nch + sub) * (nd // 2 - 1) + 1)
    ga, gw, rest_g, rest_a = pl.pallas_call(
        functools.partial(kernel, nd, nr, nc, nch, cols, sub, spare),
        out_shape=(
            pltpu.VMEM((block, feats), bf16),
            pltpu.VMEM((feats, width), bf16),
            pltpu.VMEM((TAIL, layer, cols), bf16),
            pltpu.VMEM((feats, layer), bf16),
        ),
        in_specs=[anywhere] * 3,
        out_specs=(vmem,) * 4,
        scratch_shapes=[
            pltpu.VMEM((nch, pieces * rows, cols), bf16),
            pltpu.VMEM((feats, apieces * acts.shape[0]), bf16),
            pltpu.VMEM(acts.shape, bf16),
            pltpu.VMEM((layer, feats), jnp.float32),
            pltpu.VMEM((layer, feats), bf16),
            pltpu.VMEM((nc - 1, block, feats), bf16),
            pltpu.VMEM((2, feats, cols), bf16),
            dma((pieces, nch)), dma((apieces, sub)), dma((nc - 1,)),
            dma((3 + nx - 1, pieces)), dma((2 + nc - 1, apieces)), dma((nc - 1,)),
            dma((nch + 1,)), dma((2,)),
        ],
        compiler_params=pltpu.CompilerParams(
            collective_id=0, has_side_effects=True, vmem_limit_bytes=43 << 20),
    )(acts, grad_out, weight)
    return pl.pallas_call(
        functools.partial(store, nch, spare),
        out_shape=(jax.ShapeDtypeStruct(ga.shape, bf16), jax.ShapeDtypeStruct(gw.shape, bf16)),
        in_specs=[vmem] * 4,
        out_specs=(anywhere, anywhere),
        scratch_shapes=[pltpu.VMEM((TAIL, feats, cols), bf16), dma((TAIL + STORES + 1,))],
        compiler_params=pltpu.CompilerParams(vmem_limit_bytes=6 << 20),
    )(ga, gw, rest_g, rest_a)


def solution(mesh):
    nd, nr, nc = mesh.shape["depth"], mesh.shape["row"], mesh.shape["col"]
    in_specs = (P(("depth", "col"), "row"), P(("depth", "row"), "col"), P("row", "col"))
    out_specs = (P(("depth", "col"), "row"), P("row", "col"))
    return jax.shard_map(functools.partial(shards, nd, nr, nc), mesh=mesh,
                         in_specs=in_specs, out_specs=out_specs, check_vma=False)
```

```python
import functools

import jax
import jax.numpy as jnp
from jax import lax
from jax.experimental import pallas as pl
from jax.experimental.pallas import tpu as pltpu
from jax.sharding import PartitionSpec as P

MESH = pl.DeviceIdType.MESH
CORES = 2

LEAD = 3
TAIL = 3
TILE = 256


def order(nch, spare):
    return [(i + spare) % nch for i in range(nch)]


def lag(nd, nch, sub):
    per = nch + sub
    need = [per * (d - 1) + sub + 1 - nch * d for d in range(1, nd)]
    need += [per * (nd - 2) + sub + LEAD - nch * (nd - 1) - 2]
    return max(0, 1 + max(need))


def kernel(nd, nr, nc, nch, cols, sub, spare, a_ref, g_ref, w_ref, ga_ref, gw_ref, rest_g, rest_a,
           grads, acts, own_a, total, term, parts, wbuf,
           recv_g, recv_a, recv_t, send_g, send_a, send_t, load_sem, w_sem):
    nx = nr // CORES
    l, r, c = lax.axis_index("depth"), lax.axis_index("row"), lax.axis_index("col")
    core = lax.rem(r, CORES)
    xi = lax.div(r, CORES)
    partner = xi * CORES + (1 - core)
    xpeers = [lax.rem(xi + o, nx) * CORES + core for o in range(1, nx)]
    cpeers = [lax.rem(c + o, nc) for o in range(1, nc)]
    rows = g_ref.shape[0]
    width, feats = a_ref.shape
    layer = nr * rows
    block = layer // nc
    fsub = feats // sub
    per = nch + sub
    late = lag(nd, nch, sub)
    pairs = jnp.minimum(l, nd - 1 - l)
    far_up = l < nd // 2
    last = jnp.where(far_up, nd - 1, 0)
    first = jnp.where(far_up, 0, layer)
    ends = nch * (nd - 1)
    UP, DOWN, CORE, X = 0, 1, 2, 3

    def piece(p, j):
        return grads.at[j, pl.ds(pl.multiple_of(p * rows, rows), rows), :]

    def whole(p):
        return grads.at[:, pl.ds(pl.multiple_of(p * rows, rows), rows), :]

    def apiece(q, i):
        return acts.at[pl.ds(pl.multiple_of(i * fsub, fsub), fsub), pl.ds(pl.multiple_of(q * width, width), width)]

    def awhole(q):
        return acts.at[:, pl.ds(pl.multiple_of(q * width, width), width)]

    def g_copy(p, j, way, dev):
        return pltpu.make_async_remote_copy(
            src_ref=piece(p, j), dst_ref=piece(p, j), send_sem=send_g.at[way, p],
            recv_sem=recv_g.at[p, j], device_id=dev, device_id_type=MESH)

    def a_copy(q, i, way, dev):
        return pltpu.make_async_remote_copy(
            src_ref=apiece(q, i), dst_ref=apiece(q, i), send_sem=send_a.at[way, q],
            recv_sem=recv_a.at[q, i], device_id=dev, device_id_type=MESH)

    def g_wait(p, j):
        pltpu.make_async_copy(piece(p, j), piece(p, j), recv_g.at[p, j]).wait()

    def a_wait(q, i):
        pltpu.make_async_copy(apiece(q, i), apiece(q, i), recv_a.at[q, i]).wait()

    def to_x(p, j):
        for o, dev in enumerate(xpeers):
            g_copy(p, j, X + o, {"row": dev}).start()

    def to_core(p, j):
        g_copy(p, j, CORE, {"row": partner}).start()

    def to_up(p, j):
        @pl.when(l < nd - 1)
        def _():
            g_copy(p, j, UP, {"depth": l + 1}).start()

    def to_down(p, j):
        @pl.when(l > 0)
        def _():
            g_copy(p, j, DOWN, {"depth": l - 1}).start()

    def a_up(q, i):
        @pl.when(l < nd - 1)
        def _():
            a_copy(q, i, UP, {"depth": l + 1}).start()

    def a_down(q, i):
        @pl.when(l > 0)
        def _():
            a_copy(q, i, DOWN, {"depth": l - 1}).start()

    def a_col(q, i):
        for o, dev in enumerate(cpeers):
            a_copy(q, i, 2 + o, {"col": dev}).start()

    def w_copy(j):
        return pltpu.make_async_copy(
            w_ref.at[:, pl.ds(pl.multiple_of(j * cols, cols), cols)], wbuf.at[lax.rem(j, 2)],
            w_sem.at[lax.rem(j, 2)])

    own = l * nr + r
    mine = l * nc + c

    def from_own(j):
        src = g_ref.at[:, pl.ds(pl.multiple_of(j * cols, cols), cols)]

        def send(way, dev):
            pltpu.make_async_remote_copy(
                src_ref=src, dst_ref=piece(own, j), send_sem=send_g.at[way, own],
                recv_sem=recv_g.at[own, j], device_id=dev, device_id_type=MESH).start()

        @pl.when(l < nd - 1)
        def _():
            send(UP, {"depth": l + 1})

        @pl.when(l > 0)
        def _():
            send(DOWN, {"depth": l - 1})

        for o, dev in enumerate(xpeers):
            send(X + o, {"row": dev})

    barrier = pltpu.get_barrier_semaphore()
    peers = [{"row": partner}] + [{"row": x} for x in xpeers] + [{"col": y} for y in cpeers]
    for dev in peers:
        pl.semaphore_signal(barrier, inc=1, device_id=dev, device_id_type=MESH)

    @pl.when(l > 0)
    def _():
        pl.semaphore_signal(barrier, inc=1, device_id={"depth": l - 1}, device_id_type=MESH)

    @pl.when(l < nd - 1)
    def _():
        pl.semaphore_signal(barrier, inc=1, device_id={"depth": l + 1}, device_id_type=MESH)

    @pl.loop(0, nch)
    def _(j):
        pltpu.make_async_copy(
            g_ref.at[:, pl.ds(pl.multiple_of(j * cols, cols), cols)], piece(own, j), load_sem.at[j]).start()

    own_acts = pltpu.make_async_copy(a_ref, own_a, load_sem.at[nch])
    own_acts.start()

    neighbours = jnp.where(l > 0, 1, 0) + jnp.where(l < nd - 1, 1, 0)
    pl.semaphore_wait(barrier, len(peers) + neighbours)

    for j in range(LEAD):
        from_own(j)

    own_acts.wait()
    acts[:, pl.ds(pl.multiple_of(mine * width, width), width)] = own_a[...].T

    @pl.loop(0, sub)
    def _(i):
        a_up(mine, i)
        a_down(mine, i)
        a_col(mine, i)

    @pl.loop(LEAD, nch)
    def _(j):
        from_own(j)

    @pl.loop(0, nch)
    def _(j):
        pltpu.make_async_copy(piece(own, j), piece(own, j), load_sem.at[j]).wait()
        to_core(own, j)

    for j in range(min(2, nch)):
        w_copy(j).start()

    total[...] = jnp.zeros_like(total)

    def tiles(body):
        @pl.loop(0, feats // TILE)
        def _(i):
            body(pl.ds(pl.multiple_of(i * TILE, TILE), TILE))

    def core_wait(k, j):
        for x in range(nx):
            g_wait(k * nr + x * CORES + 1 - core, j)

    def sent_g(way, p):
        pltpu.make_async_copy(whole(p), whole(p), send_g.at[way, p]).wait()

    def sent_one(way, p):
        pltpu.make_async_copy(piece(p, 0), piece(p, 0), send_g.at[way, p]).wait()

    def sent_a(way, q):
        pltpu.make_async_copy(awhole(q), awhole(q), send_a.at[way, q]).wait()

    def sent(k, pieces):
        p, q = k * nr + r, k * nc + c

        @pl.when((k <= l) & (l < nd - 1))
        def _():
            sent_g(UP, p)
            sent_a(UP, q)

        @pl.when((k >= l) & (l > 0))
        def _():
            sent_g(DOWN, p)
            sent_a(DOWN, q)

        part = grads.at[pl.ds(0, pieces), pl.ds(pl.multiple_of(p * rows, rows), rows), :]
        for o in range(len(xpeers)):
            pltpu.make_async_copy(part, part, send_g.at[X + o, p]).wait()
        for x in range(nx):
            sent_g(CORE, k * nr + x * CORES + core)
        for o in range(len(cpeers)):
            sent_a(2 + o, q)

    def step(t, carry):
        z = t - 1
        dist = lax.div(z, per) + 1
        v = lax.rem(z, per)
        turn = jnp.where((dist == nd - 1) & (nd > 2), spare, 0)
        lead = LEAD - turn
        is_a = (v >= lead) & (v < lead + sub)
        jz = jnp.where(v < lead, v, v - sub) + turn
        jz = jnp.where(jz < nch, jz, 0)
        for sign, g_on, a_on in ((-1, to_up, a_up), (1, to_down, a_down)):
            src = l + sign * dist
            there = (z >= 0) & (dist < nd) & (src >= 0) & (src < nd)

            @pl.when(there & ~is_a)
            def _(p=src * nr + r, g_on=g_on, src=src, sign=sign):
                g_wait(p, jz)
                if spare:
                    kept = (src == last) & (jz == 0)

                    @pl.when(~(kept & ((l == nd - 2) if sign < 0 else (l == 1))))
                    def _():
                        g_on(p, jz)

                    @pl.when(~kept)
                    def _():
                        to_x(p, jz)
                else:
                    g_on(p, jz)
                    to_x(p, jz)
                to_core(p, jz)

            @pl.when(there & is_a)
            def _(q=src * nc + c, i=v - lead, a_on=a_on):
                a_wait(q, i)
                a_on(q, i)
                a_col(q, i)

        if spare:
            p = last * nr + xpeers[0]

            @pl.when((t == per * (nd - 1 - l) + 1) & far_up)
            def _():
                @pl.when(l == 1)
                def _():
                    to_down(last * nr + r, 0)

                g_wait(p, 0)
                to_down(p, 0)
                to_core(p, 0)

            @pl.when((t == per * l + 1) & ~far_up)
            def _():
                @pl.when(l == nd - 2)
                def _():
                    to_up(last * nr + r, 0)

                g_wait(p, 0)
                to_up(p, 0)
                to_core(p, 0)

            @pl.when((t == per * (nd // 2 - 1) + 1) & (l == nd // 2))
            def _():
                to_down((nd - 1) * nr + xpeers[0], 0)

            @pl.when((t == per * (nd // 2 - 1) + 1) & (l == nd // 2 - 1))
            def _():
                to_up(xpeers[0], 0)

        ja = t - late - 2

        @pl.when((ja >= 0) & (ja < nch))
        def _():
            core_wait(l, ja)
            w_copy(ja).wait()
            lhs = grads[ja, pl.ds(pl.multiple_of(l * layer, layer), layer), :]

            def body(at):
                total[:, at] += lax.dot_general(
                    lhs, wbuf[lax.rem(ja, 2), at, :], (((1,), (1,)), ((), ())),
                    preferred_element_type=jnp.float32)

            tiles(body)

            @pl.when(ja + 2 < nch)
            def _():
                w_copy(ja + 2).start()

        @pl.when(ja == nch)
        def _():
            term[...] = total[...].astype(term.dtype)
            for o, dev in enumerate(cpeers):
                pltpu.make_async_remote_copy(
                    src_ref=term.at[pl.ds(pl.multiple_of(dev * block, block), block), :],
                    dst_ref=parts.at[o], send_sem=send_t.at[o], recv_sem=recv_t.at[o],
                    device_id={"col": dev}, device_id_type=MESH).start()

        @pl.when(ja == nch + 8)
        def _():
            result = total[pl.ds(pl.multiple_of(c * block, block), block), :]
            for o in range(len(cpeers)):
                pltpu.make_async_copy(parts.at[o], parts.at[o], recv_t.at[o]).wait()
                result = result + parts[o].astype(jnp.float32)
            ga_ref[...] = result.astype(ga_ref.dtype)
            for o in range(len(cpeers)):
                pltpu.make_async_copy(parts.at[o], parts.at[o], send_t.at[o]).wait()

        jb = ja - nch * (nd - 2)

        @pl.when(jb == 0)
        def _():
            for k in range(nd):
                @pl.when(k != last)
                def _(k=k):
                    for dev in cpeers:
                        for i in range(sub):
                            a_wait(k * nc + dev, i)

        @pl.when((jb >= 0) & (jb < nch))
        def _():
            for k in range(nd):
                @pl.when((k != last) & (k != l))
                def _(k=k):
                    core_wait(k, jb)

            tokens = pl.ds(pl.multiple_of(first, layer), (nd - 1) * layer)

            def body(at):
                gw_ref[at, pl.ds(pl.multiple_of(jb * cols, cols), cols)] = jnp.dot(
                    acts[at, tokens], grads[jb, tokens, :], preferred_element_type=jnp.float32).astype(gw_ref.dtype)

            tiles(body)

        jc = jb - nch

        @pl.when(jc == 4)
        def _():
            rest_a[...] = acts[:, pl.ds(pl.multiple_of(last * layer, layer), layer)]
            for k in range(nd):
                @pl.when(k != last)
                def _(k=k):
                    sent(k, nch)

        @pl.when(jc == 0)
        def _():
            for dev in cpeers:
                for i in range(sub):
                    a_wait(last * nc + dev, i)

        @pl.when((jc >= 0) & (jc < nch - TAIL))
        def _():
            j = lax.rem(jc + spare, nch)
            core_wait(last, j)
            tokens = pl.ds(pl.multiple_of(last * layer, layer), layer)

            def body(at):
                here = pl.ds(pl.multiple_of(j * cols, cols), cols)
                gw_ref[at, here] = (gw_ref[at, here].astype(jnp.float32) + jnp.dot(
                    acts[at, tokens], grads[j, tokens, :], preferred_element_type=jnp.float32)).astype(gw_ref.dtype)

            tiles(body)

        @pl.when((jc >= nch - TAIL) & (jc < nch - 2))
        def _():
            j = lax.rem(jc + spare, nch)
            core_wait(last, j)
            rest_g[jc - (nch - TAIL)] = grads[j, pl.ds(pl.multiple_of(last * layer, layer), layer), :]

        u = t - late
        if spare:
            u = jnp.where(u >= ends, u + 1, u)
        e = u - nch
        paired = e < 2 * nch * pairs
        e2 = e - 2 * nch * pairs
        dist = jnp.where(paired, lax.div(e, 2 * nch), pairs + lax.div(e2, nch)) + 1
        j = jnp.where(paired, lax.div(lax.rem(e, 2 * nch), 2), lax.rem(e2, nch))
        up = jnp.where(paired, lax.rem(e, 2) == 1, far_up)
        src = jnp.where(e < 0, l, jnp.where(up, l + dist, l - dist))
        j = jnp.where(e < 0, u, j)

        @pl.when((u >= 0) & (u < nch * nd))
        def _():
            for x in xpeers:
                g_wait(src * nr + x, j)
                to_core(src * nr + x, j)

        return carry

    lax.fori_loop(0, nch * nd + late, step, 0)
    for i, j in list(enumerate(order(nch, spare)[nch - TAIL:]))[-2:]:
        core_wait(last, j)
        rest_g[i] = grads[j, pl.ds(pl.multiple_of(last * layer, layer), layer), :]

    sent(last, nch - spare)

    if spare:
        p = last * nr + xpeers[0]

        @pl.when((l > 0) & far_up)
        def _():
            sent_one(DOWN, p)

        @pl.when((l < nd - 1) & ~far_up)
        def _():
            sent_one(UP, p)

        @pl.when(l == nd // 2)
        def _():
            sent_one(DOWN, (nd - 1) * nr + xpeers[0])

        @pl.when(l == nd // 2 - 1)
        def _():
            sent_one(UP, xpeers[0])


def store(nch, spare, ga_ref, gw_ref, rest_g, rest_a, ga_out, gw_out, rest, sem):
    feats, cols = gw_ref.shape[0], rest_g.shape[2]
    done = [j for i, j in enumerate(order(nch, spare)) if i < nch - TAIL]
    whole = pl.ds(min(done) * cols, len(done) * cols)
    copies = [pltpu.make_async_copy(gw_ref.at[:, whole], gw_out.at[:, whole], sem.at[TAIL]),
              pltpu.make_async_copy(ga_ref, ga_out, sem.at[TAIL + 1])]
    for copy in copies:
        copy.start()
    for i, j in enumerate(order(nch, spare)[nch - TAIL:]):
        here = pl.ds(j * cols, cols)

        @pl.loop(0, feats // TILE)
        def _(k):
            f = pl.ds(pl.multiple_of(k * TILE, TILE), TILE)
            rest[i, f, :] = (gw_ref[f, here].astype(jnp.float32) + jnp.dot(
                rest_a[f, :], rest_g[i], preferred_element_type=jnp.float32)).astype(rest.dtype)

        copies.append(pltpu.make_async_copy(rest.at[i], gw_out.at[:, here], sem.at[i]))
        copies[-1].start()
    for copy in copies:
        copy.wait()


def shards(nd, nr, nc, acts, grad_out, weight):
    rows, width = grad_out.shape
    cols = 512 if width % 512 == 0 else 256
    nch = width // cols
    feats = acts.shape[1]
    layer = nr * rows
    block = layer // nc
    bf16, dma = jnp.bfloat16, pltpu.SemaphoreType.DMA
    anywhere = pl.BlockSpec(memory_space=pl.ANY)
    vmem = pl.BlockSpec(memory_space=pltpu.VMEM)
    nx = nr // CORES
    pieces, apieces = nd * nr, nd * nc
    sub = max(1, acts.size // (rows * cols))
    spare = int(nx == 2 and nd > 2 and
                nch * (nd - 3) + 1 + lag(nd, nch, sub) < (nch + sub) * (nd // 2 - 1) + 1)
    ga, gw, rest_g, rest_a = pl.pallas_call(
        functools.partial(kernel, nd, nr, nc, nch, cols, sub, spare),
        out_shape=(
            pltpu.VMEM((block, feats), bf16),
            pltpu.VMEM((feats, width), bf16),
            pltpu.VMEM((TAIL, layer, cols), bf16),
            pltpu.VMEM((feats, layer), bf16),
        ),
        in_specs=[anywhere] * 3,
        out_specs=(vmem,) * 4,
        scratch_shapes=[
            pltpu.VMEM((nch, pieces * rows, cols), bf16),
            pltpu.VMEM((feats, apieces * acts.shape[0]), bf16),
            pltpu.VMEM(acts.shape, bf16),
            pltpu.VMEM((layer, feats), jnp.float32),
            pltpu.VMEM((layer, feats), bf16),
            pltpu.VMEM((nc - 1, block, feats), bf16),
            pltpu.VMEM((2, feats, cols), bf16),
            dma((pieces, nch)), dma((apieces, sub)), dma((nc - 1,)),
            dma((3 + nx - 1, pieces)), dma((2 + nc - 1, apieces)), dma((nc - 1,)),
            dma((nch + 1,)), dma((2,)),
        ],
        compiler_params=pltpu.CompilerParams(
            collective_id=0, has_side_effects=True, vmem_limit_bytes=43 << 20),
    )(acts, grad_out, weight)
    return pl.pallas_call(
        functools.partial(store, nch, spare),
        out_shape=(jax.ShapeDtypeStruct(ga.shape, bf16), jax.ShapeDtypeStruct(gw.shape, bf16)),
        in_specs=[vmem] * 4,
        out_specs=(anywhere, anywhere),
        scratch_shapes=[pltpu.VMEM((TAIL, feats, cols), bf16), dma((TAIL + 2,))],
        compiler_params=pltpu.CompilerParams(vmem_limit_bytes=6 << 20),
    )(ga, gw, rest_g, rest_a)


def solution(mesh):
    nd, nr, nc = mesh.shape["depth"], mesh.shape["row"], mesh.shape["col"]
    in_specs = (P(("depth", "col"), "row"), P(("depth", "row"), "col"), P("row", "col"))
    out_specs = (P(("depth", "col"), "row"), P("row", "col"))
    return jax.shard_map(functools.partial(shards, nd, nr, nc), mesh=mesh,
                         in_specs=in_specs, out_specs=out_specs, check_vma=False)
```
